768 devices in a mesh: elem: 96 (over y, z), clus: 8 (over x, core).
Axes of the slice: x: 4, y: 8, z: 12, core: 2. Of those that a mesh axis runs over, the one named last changes fastest.
Arguments:
- nodal: float32 [512, 196608], P(None, ('elem', 'clus')), may hold values from -6 to 6
- metric: bfloat16 [3, 512, 196608], P(None, None, ('elem', 'clus')), may hold values from 0.25 to 2.5
- derivative: float32 [8, 8], replicated, may hold values from -2 to 2
- interp: float32 [2, 8, 8], replicated, may hold values from -2 to 2
- face_level: int32 [1179648], P(('elem', 'clus')), may hold values from 0 to 4
- face_target: int32 [1179648], P(('elem', 'clus')), may hold values from 0 to 895, as said below
- slot_mortar: int32 [294912], P(('elem', 'clus')), may hold values from 0 to 511
- vertex_ids: int32 [8, 196608], P(None, ('elem', 'clus')), may hold values from 0 to 24575, as said below
Outputs:
- applied: float32 [512, 196608], P(None, ('elem', 'clus'))
The draws below stay inside these ranges and needn't reach their ends.
Inputs may be any that keep to these rules, and one draw needn't show every extreme that they name: `face_target`: A value below 512 names a mortar of the face's own device; a value 512 + s names slot s of that device's outgoing buffer, laid out as in the reference program. No two faces of one device name the same slot, and on some device every slot is named. `vertex_ids`: the coarse vertices of the elements on elem index e lie in e * 256 to e * 256 + 2 * 256 - 1, taken modulo 24576.
All inputs are finite; a program needn't handle non-finite values.
Results may differ from the reference program's by a relative error of at most 0.0003.
Values sent between devices are 32-bit elements; how exact they have to be, the bound alone decides.
A program may use at most 32 MiB of HBM per device.

```python
import math
import jax
import jax.numpy as jnp
from jax import lax

POINTS = 8
E_DEV = 256
CAP_E = 128
CAP_C = 16
GROUP = 8
SLOTS = 384
M_DEV = 512
NV_DEV = 256
NV = 24576
ELEMENTS = 196608
FACES = 1179648
SLOTS_ALL = 294912
N_ELEM = 96
N_CLUS = 8


def one_device(key, fill_level):
    key_used, key_order, key_local = jax.random.split(key, 3)
    slot_used = jax.random.randint(key_used, (SLOTS,), 0, 4) < fill_level
    slot_order = jnp.argsort(jnp.where(slot_used, 0, SLOTS) + jnp.arange(SLOTS))
    used_count = jnp.sum(slot_used.astype(jnp.int32))
    face_order = jax.random.permutation(key_order, 6 * E_DEV)
    face_rank = jnp.argsort(face_order)
    local_mortar = jax.random.randint(key_local, (6 * E_DEV,), 0, M_DEV)
    sent_slot = M_DEV + slot_order[jnp.minimum(face_rank, SLOTS - 1)]
    return jnp.where(face_rank < used_count, sent_slot, local_mortar).astype(jnp.int32)


def draw_face_target(key, part):
    devices = ELEMENTS // E_DEV
    key_fill, key_full, key_each = jax.random.split(key, 3)
    fill_level = jax.random.randint(key_fill, (devices,), 1, 5)
    full_device = jax.random.randint(key_full, (), 0, devices)
    fill_level = jnp.where(jnp.arange(devices) == full_device, 4, fill_level)
    return jax.vmap(one_device)(jax.random.split(key_each, devices), fill_level).reshape(-1)


def draw_vertex_ids(key, part):
    positions = jnp.arange(ELEMENTS)
    elem_of = positions // E_DEV // GROUP
    offsets = jax.random.randint(key, (8, ELEMENTS), 0, 2 * NV_DEV)
    first_one = positions % E_DEV == 0
    offsets = offsets.at[0].set(jnp.where(first_one, 2 * NV_DEV - 1, offsets[0]))
    offsets = offsets.at[1].set(jnp.where(first_one, 0, offsets[1]))
    return jnp.mod(elem_of[None, :] * NV_DEV + offsets, NV).astype(jnp.int32)


def plant(values, key, least, high):
    extent = values.shape
    spot = [jax.random.randint(jax.random.fold_in(key, axis), (), 0, extent[axis]) for axis in range(len(extent))]
    values = values.at[tuple(spot)].set(least)
    longest = extent.index(max(extent))
    spot[longest] = (spot[longest] + 1) % extent[longest]
    return values.at[tuple(spot)].set(high)


def level_of(own_key, dims, pieces, least, top_value):
    def one(position, blocks):
        steps = jax.random.uniform(jax.random.fold_in(jax.random.fold_in(own_key, 6), position), (blocks,), jnp.float32, least / len(pieces), top_value / len(pieces))
        return jnp.repeat(jnp.exp(steps), dims[position] // blocks).reshape((-1,) + (1,) * (len(dims) - position - 1))

    gain = one(*pieces[0])
    for cut in pieces[1:]:
        gain = gain * one(*cut)
    return gain


def scatter_about(key, extent, scale, bound, cuts=(), kind=jnp.bfloat16):
    values = jax.random.normal(key, extent, jnp.float32) * scale
    if len(cuts) > 0:
        values = level_of(key, extent, cuts, -0.22, 0.18) * values
    return jnp.clip(values, min=-bound, max=bound).astype(kind)


def setup_inputs(seed: int = 0) -> dict:
    streams_of = jax.random.split(jax.random.key(seed), 9)
    nodal = scatter_about(streams_of[0], (POINTS ** 3, ELEMENTS), 1.0, 6.0, ((1, 768),), jnp.float32)
    metric = jnp.clip(jnp.exp(math.log(2.5) - 2.3025851 * jax.random.uniform(streams_of[1], (3, POINTS ** 3, ELEMENTS), jnp.float32) ** level_of(streams_of[1], (3, POINTS ** 3, ELEMENTS), ((2, 768),), -0.2, 0.2)), 0.25, 2.5).astype(jnp.bfloat16)
    derivative = scatter_about(streams_of[2], (POINTS, POINTS), POINTS ** -0.5, 2.0, (), jnp.float32)
    interp = scatter_about(streams_of[3], (2, POINTS, POINTS), POINTS ** -0.5, 2.0, (), jnp.float32)
    face_level = plant(jax.random.randint(streams_of[4], (FACES,), 0, 5), jax.random.fold_in(streams_of[4], 1), 0, 4).astype(jnp.int32)
    face_target = draw_face_target(jax.random.fold_in(streams_of[8], 71), 0)
    slot_mortar = plant(jax.random.randint(streams_of[6], (SLOTS_ALL,), 0, M_DEV), jax.random.fold_in(streams_of[6], 1), 0, M_DEV - 1).astype(jnp.int32)
    vertex_ids = draw_vertex_ids(jax.random.fold_in(streams_of[8], 71), 0)
    return {"nodal": nodal, "metric": metric, "derivative": derivative, "interp": interp, "face_level": face_level, "face_target": face_target, "slot_mortar": slot_mortar, "vertex_ids": vertex_ids}


highest = lax.Precision.HIGHEST


def face_traces(nodal_block, points):
    element_cube = nodal_block.reshape(points, points, points, -1)
    far_index = points - 1
    slab_list = [element_cube[0], element_cube[far_index], element_cube[:, 0], element_cube[:, far_index], element_cube[:, :, 0], element_cube[:, :, far_index]]
    return jnp.concatenate(slab_list, axis=2)


def face_maps(interp, face_level, points):
    identity = jnp.eye(points, dtype=jnp.float32)[:, :, None]
    first_one = interp[0][:, :, None]
    second_one = interp[1][:, :, None]
    level_row = face_level[None, None, :]
    left_map = jnp.where(level_row == 0, identity, jnp.where(level_row <= 2, first_one, second_one))
    right_map = jnp.where(level_row == 0, identity, jnp.where(level_row % 2 == 1, first_one, second_one))
    return left_map, right_map


def project_traces(traces, left_map, right_map):
    partial_rows = jnp.einsum('xaf,abf->xbf', left_map, traces, precision=highest)
    return jnp.einsum('ybf,xbf->xyf', right_map, partial_rows, precision=highest)


def back_project(values, left_map, right_map):
    partial_rows = jnp.einsum('xaf,xyf->ayf', left_map, values, precision=highest)
    return jnp.einsum('ybf,ayf->abf', right_map, partial_rows, precision=highest)


def stiffness_apply(nodal_block, metric_block, derivative, points):
    element_cube = nodal_block.reshape(points, points, points, -1)
    metric_cube = metric_block.astype(jnp.float32).reshape(3, points, points, points, -1)
    grad_first = jnp.einsum('ai,ijke->ajke', derivative, element_cube, precision=highest)
    grad_second = jnp.einsum('bj,ijke->ibke', derivative, element_cube, precision=highest)
    grad_third = jnp.einsum('ck,ijke->ijce', derivative, element_cube, precision=highest)
    result = jnp.einsum('ai,ajke->ijke', derivative, metric_cube[0] * grad_first, precision=highest)
    result = result + jnp.einsum('bj,ibke->ijke', derivative, metric_cube[1] * grad_second, precision=highest)
    result = result + jnp.einsum('ck,ijce->ijke', derivative, metric_cube[2] * grad_third, precision=highest)
    return result


def corner_values(nodal_block, points):
    element_cube = nodal_block.reshape(points, points, points, -1)
    far_index = points - 1
    return jnp.stack([element_cube[(corner // 4) * far_index, ((corner // 2) % 2) * far_index, (corner % 2) * far_index] for corner in range(8)])


def finish_block(result_cube, back_faces, corner_fix, points):
    far_index = points - 1
    count_elems = result_cube.shape[-1]
    face_parts = back_faces.reshape(points, points, 6, count_elems)
    result_cube = result_cube.at[0].add(face_parts[:, :, 0])
    result_cube = result_cube.at[far_index].add(face_parts[:, :, 1])
    result_cube = result_cube.at[:, 0].add(face_parts[:, :, 2])
    result_cube = result_cube.at[:, far_index].add(face_parts[:, :, 3])
    result_cube = result_cube.at[:, :, 0].add(face_parts[:, :, 4])
    result_cube = result_cube.at[:, :, far_index].add(face_parts[:, :, 5])
    for corner in range(8):
        result_cube = result_cube.at[(corner // 4) * far_index, ((corner // 2) % 2) * far_index, (corner % 2) * far_index].add(corner_fix[corner])
    return result_cube.reshape(points ** 3, count_elems)


def regroup(blocks, width_sq):
    shaped = blocks.reshape(N_ELEM, N_CLUS, width_sq, N_CLUS, CAP_C)
    return shaped.transpose(0, 3, 2, 1, 4).reshape(N_ELEM, N_CLUS, width_sq, N_CLUS * CAP_C)


def assemble(local_cols, incoming_cols, slot_row):
    mortar = local_cols.at[:, slot_row].add(incoming_cols)
    return mortar, mortar[:, slot_row]


def reference(nodal, metric, derivative, interp, face_level, face_target, slot_mortar, vertex_ids):
    devices = N_ELEM * N_CLUS
    points = POINTS
    width_sq = points * points
    per_face = 6 * E_DEV

    def send_one(device_index):
        first_col = (device_index * E_DEV).astype(jnp.int32)
        first_face = (device_index * per_face).astype(jnp.int32)
        nodal_block = lax.dynamic_slice_in_dim(nodal, first_col, E_DEV, axis=1)
        level_row = lax.dynamic_slice_in_dim(face_level, first_face, per_face)
        target_row = lax.dynamic_slice_in_dim(face_target, first_face, per_face)
        left_map, right_map = face_maps(interp, level_row, points)
        projected = project_traces(face_traces(nodal_block, points), left_map, right_map)
        return jnp.zeros((width_sq, M_DEV + SLOTS), jnp.float32).at[:, target_row].add(projected.reshape(width_sq, -1))

    outgoing = lax.map(send_one, jnp.arange(devices, dtype=jnp.int32))
    grid = outgoing.reshape(N_ELEM, N_CLUS, width_sq, M_DEV + SLOTS)
    local_part = grid[..., :M_DEV]
    to_prev = grid[..., M_DEV:M_DEV + CAP_E]
    to_next = grid[..., M_DEV + CAP_E:M_DEV + 2 * CAP_E]
    to_group = grid[..., M_DEV + 2 * CAP_E:]
    incoming = jnp.concatenate([jnp.roll(to_next, 1, axis=0), jnp.roll(to_prev, -1, axis=0), regroup(to_group, width_sq)], axis=3)
    slot_grid = slot_mortar.reshape(N_ELEM, N_CLUS, SLOTS)
    mortar, answers = jax.vmap(jax.vmap(assemble))(local_part, incoming, slot_grid)
    returned = jnp.concatenate([mortar, jnp.roll(answers[..., CAP_E:2 * CAP_E], 1, axis=0), jnp.roll(answers[..., :CAP_E], -1, axis=0), regroup(answers[..., 2 * CAP_E:], width_sq)], axis=3)
    returned_dev = returned.reshape(devices, width_sq, M_DEV + SLOTS)

    corners_all = corner_values(nodal, points)
    flat_ids = vertex_ids.reshape(-1)
    totals = jnp.zeros((NV,), jnp.float32).at[flat_ids].add(corners_all.reshape(-1))
    counts = jnp.zeros((NV,), jnp.float32).at[flat_ids].add(jnp.ones(flat_ids.shape, jnp.float32))
    coarse = totals / (1.0 + counts)
    corner_fix = coarse[vertex_ids]

    def finish_one(device_index):
        first_col = (device_index * E_DEV).astype(jnp.int32)
        first_face = (device_index * per_face).astype(jnp.int32)
        nodal_block = lax.dynamic_slice_in_dim(nodal, first_col, E_DEV, axis=1)
        metric_block = lax.dynamic_slice_in_dim(metric, first_col, E_DEV, axis=2)
        fix_block = lax.dynamic_slice_in_dim(corner_fix, first_col, E_DEV, axis=1)
        level_row = lax.dynamic_slice_in_dim(face_level, first_face, per_face)
        target_row = lax.dynamic_slice_in_dim(face_target, first_face, per_face)
        left_map, right_map = face_maps(interp, level_row, points)
        picked = returned_dev[device_index][:, target_row].reshape(points, points, -1)
        back_faces = back_project(picked, left_map, right_map)
        result_cube = stiffness_apply(nodal_block, metric_block, derivative, points)
        return finish_block(result_cube, back_faces, fix_block, points)

    blocks = lax.map(finish_one, jnp.arange(devices, dtype=jnp.int32))
    return blocks.transpose(1, 0, 2).reshape(points ** 3, devices * E_DEV)
```

```python
import functools

import jax
import jax.numpy as jnp
from jax import lax
from jax.experimental import pallas as pl
from jax.experimental.pallas import tpu as pltpu
from jax.sharding import PartitionSpec as P

CAP_E = 128
CAP_C = 16
GROUP = 8
M_DEV = 512
SLOTS = 2 * CAP_E + GROUP * CAP_C
COLS = M_DEV + SLOTS
NV_DEV = 256
E_DEV = 256
FACES = 6 * E_DEV
NODES = 512
MESH = pl.DeviceIdType.MESH
F32 = jnp.float32
BF16 = jnp.bfloat16

NT = (((1,), (1,)), ((), ()))
NN = (((1,), (0,)), ((), ()))


def mm(a, b, dims=NN):
    return lax.dot_general(a, b, dims, preferred_element_type=F32)


def split(x):
    hi = x.astype(BF16)
    return hi, (x - hi.astype(F32)).astype(BF16)


def stacked(x):
    hi, lo = split(x)
    return jnp.concatenate([hi, lo, hi], axis=0)


def halves(x):
    return x[:64] + x[64:]


def iota(shape, axis):
    return lax.broadcasted_iota(jnp.int32, shape, axis)


def three_terms(full):
    hi = full.astype(BF16).astype(F32)
    lane = iota(full.shape, 1)
    return jnp.where(lane < 128, hi, full - hi).astype(BF16)


def kernel(
    n_elem,
    u_hbm,
    met_hbm,
    ma_hbm,
    mb_hbm,
    lvl_hbm,
    tgt_hbm,
    slot_hbm,
    vid_hbm,
    out,
    u,
    met,
    ma,
    mb,
    lvl,
    tgt,
    slot,
    vid,
    pick,
    pick2,
    corner_hot,
    proj,
    own,
    picked,
    grad0,
    acc,
    send_e,
    send_g,
    recv_e,
    recv_g,
    send_e2,
    send_g2,
    recv_e2,
    recv_g2,
    in_sem,
    se_sem,
    re_sem,
    sg_sem,
    rg_sem,
    se2_sem,
    re2_sem,
    sg2_sem,
    rg2_sem,
):
    e = lax.axis_index("elem")
    c = lax.axis_index("clus")
    nxt = lax.rem(e + 1, n_elem)
    prv = lax.rem(e + n_elem - 1, n_elem)

    loads = [
        pltpu.make_async_copy(src, dst, in_sem.at[n])
        for n, (src, dst) in enumerate(
            [
                (tgt_hbm, tgt),
                (u_hbm.at[:, 0:128], u.at[0]),
                (u_hbm.at[:, 128:256], u.at[1]),
                (ma_hbm, ma),
                (mb_hbm, mb),
                (lvl_hbm, lvl),
                (vid_hbm, vid),
                (slot_hbm, slot),
                (met_hbm, met),
            ]
        )
    ]
    for load in loads:
        load.start()

    def node_rows(ref, place):
        return jnp.concatenate([ref[0, place, :], ref[1, place, :]], axis=1)

    def add_rows(place, value):
        for side in range(2):
            acc[side, place, :] = acc[side, place, :] + value[:, 128 * side : 128 * side + 128]

    barrier = pltpu.get_barrier_semaphore()
    for peer in (nxt, prv):
        pl.semaphore_signal(barrier, inc=1, device_id={"elem": peer}, device_id_type=MESH)
    for k in range(1, GROUP):
        peer = lax.rem(c + k, GROUP)
        pl.semaphore_signal(barrier, inc=1, device_id={"clus": peer}, device_id_type=MESH)

    loads[0].wait()
    rows = iota((COLS, 128), 0)
    for b in range(FACES // 128):
        hot = jnp.where(rows == tgt[b : b + 1, :], 1.0, 0.0).astype(BF16)
        pick[:, b * 128 : (b + 1) * 128] = hot

    loads[3].wait()
    loads[4].wait()

    def kron(first, second):
        return jnp.concatenate(
            [
                jnp.broadcast_to(ma[8 * first + x : 8 * first + x + 1, :], (8, 192))
                * mb[8 * second : 8 * second + 8, :]
                for x in range(8)
            ],
            axis=0,
        )

    def first_kron(which):
        full = jnp.concatenate(
            [
                jnp.broadcast_to(ma[8 * which + x : 8 * which + x + 1, :], (8, 192))
                for x in range(8)
            ],
            axis=0,
        )
        keep = (iota((64, 192), 0) & 7) == (iota((64, 192), 1) & 7)
        return jnp.where(keep, full, 0.0)

    def second_kron(which):
        full = jnp.concatenate([mb[8 * which : 8 * which + 8, :]] * 8, axis=0)
        keep = (iota((64, 192), 0) >> 3) == ((iota((64, 192), 1) & 63) >> 3)
        return jnp.where(keep, full, 0.0)

    pairs = [(0, 0), (0, 1), (1, 0), (1, 1)]
    forth = three_terms(jnp.concatenate([kron(r, s) for r, s in pairs], axis=0))

    loads[1].wait()
    loads[2].wait()
    loads[5].wait()
    for f in range(6):
        if f == 0:
            trace = node_rows(u, slice(0, 64))
        elif f == 1:
            trace = node_rows(u, slice(448, 512))
        elif f == 2:
            trace = jnp.concatenate([node_rows(u, slice(64 * i, 64 * i + 8)) for i in range(8)], axis=0)
        elif f == 3:
            trace = jnp.concatenate(
                [node_rows(u, slice(64 * i + 56, 64 * i + 64)) for i in range(8)], axis=0
            )
        else:
            first = 0 if f == 4 else 7
            trace = node_rows(u, pl.ds(first, 64, stride=8))
        level = jnp.concatenate([lvl[2 * f : 2 * f + 1, :], lvl[2 * f + 1 : 2 * f + 2, :]], axis=1)
        level = jnp.broadcast_to(level, (64, E_DEV))
        every = mm(forth, stacked(trace))
        chosen = trace
        for n in range(4):
            chosen = jnp.where(level == n + 1, every[64 * n : 64 * n + 64], chosen)
        hi, lo = split(chosen)
        proj[0:64, f * 256 : (f + 1) * 256] = hi
        proj[64:128, f * 256 : (f + 1) * 256] = lo

    loads[6].wait()
    away = vid[...] - e * NV_DEV
    total_vertices = n_elem * NV_DEV
    window = jnp.where(away < 0, away + total_vertices, away)
    high = window >> 6
    low = window & 63
    sums = jnp.zeros((32, 128), F32)
    eight = iota((8, E_DEV), 0)
    lanes_rows = iota((128, E_DEV), 0) - 64
    for corner in range(8):
        row = 7 * (64 * (corner // 4) + 8 * (corner // 2 % 2) + corner % 2)
        value = jnp.broadcast_to(node_rows(u, slice(row, row + 1)), (8, E_DEV))
        hi = value.astype(BF16).astype(F32)
        here = eight == high[corner : corner + 1, :]
        parts = [
            jnp.where(here, hi, 0.0),
            jnp.where(here, value - hi, 0.0),
            jnp.where(here, 1.0, 0.0),
            jnp.zeros((8, E_DEV), F32),
        ]
        hot = jnp.where(lanes_rows == low[corner : corner + 1, :], 1.0, 0.0).astype(BF16)
        corner_hot[:, corner * 256 : (corner + 1) * 256] = hot
        sums = sums + mm(jnp.concatenate(parts, axis=0).astype(BF16), hot, NT)
    local = jnp.concatenate([sums[0:8] + sums[8:16], sums[16:24]], axis=0)

    leaving = halves(mm(proj[...], pick[M_DEV:COLS, :], NT))
    send_e[0] = leaving[:, 0:128]
    send_e[1] = leaving[:, 128:256]
    turned = jnp.concatenate([leaving[:, 256:384], jnp.zeros((64, 128), F32)], axis=0).T
    send_g[...] = turned + jnp.concatenate([local] * GROUP, axis=0)

    def edge_copies(src, dst, ssem, rsem):
        return [
            pltpu.make_async_remote_copy(
                src.at[way],
                dst.at[1 - way],
                ssem.at[way],
                rsem.at[1 - way],
                device_id={"elem": peer},
                device_id_type=MESH,
            )
            for way, peer in ((0, prv), (1, nxt))
        ]

    def group_copies(src, dst, ssem, rsem, rows):
        copies = []
        for k in range(1, GROUP):
            peer = lax.rem(c + k, GROUP)
            copies.append(
                pltpu.make_async_remote_copy(
                    src.at[pl.ds(pl.multiple_of(peer * rows, rows), rows), :],
                    dst.at[pl.ds(pl.multiple_of(c * rows, rows), rows), :],
                    ssem.at[k - 1],
                    rsem.at[k - 1],
                    device_id={"clus": peer},
                    device_id_type=MESH,
                )
            )
        return copies

    pl.semaphore_wait(barrier, GROUP + 1)
    first_round = edge_copies(send_e, recv_e, se_sem, re_sem)
    first_round += group_copies(send_g, recv_g, sg_sem, rg_sem, CAP_C)
    for copy in first_round:
        copy.start()
    mine = pl.ds(pl.multiple_of(c * CAP_C, CAP_C), CAP_C)
    recv_g[mine, :] = send_g[mine, :]

    own[...] = halves(mm(proj[...], pick[0:M_DEV, :], NT))
    loads[7].wait()
    rows2 = iota((M_DEV, 128), 0)
    for b in range(SLOTS // 128):
        hot = jnp.where(rows2 == slot[b : b + 1, :], 1.0, 0.0).astype(BF16)
        pick2[:, b * 128 : (b + 1) * 128] = hot

    loads[8].wait()
    d_first = first_kron(2)
    d_second = second_kron(2)
    fore12 = three_terms(jnp.concatenate([d_first, d_second], axis=0))
    fore0 = fore12[0:64]
    t_first = three_terms(first_kron(5))
    t_second = three_terms(second_kron(5))
    for j in range(8):
        part = jnp.concatenate(
            [node_rows(u, slice(64 * i + 8 * j, 64 * i + 8 * j + 8)) for i in range(8)], axis=0
        )
        grad = mm(fore0, stacked(part))
        for i in range(8):
            grad0[64 * i + 8 * j : 64 * i + 8 * j + 8, :] = grad[8 * i : 8 * i + 8]
    for i in range(8):
        block = slice(64 * i, 64 * i + 64)
        grad = mm(fore12, stacked(node_rows(u, block)))
        flow1 = met[1, block, :].astype(F32) * grad[0:64]
        flow2 = met[2, block, :].astype(F32) * grad[64:128]
        grad0[block, :] = met[0, block, :].astype(F32) * grad0[block, :]
        back = mm(t_first, stacked(flow1)) + mm(t_second, stacked(flow2))
        acc[0, block, :] = back[:, 0:128]
        acc[1, block, :] = back[:, 128:256]
    for j in range(8):
        part = jnp.concatenate(
            [grad0[64 * i + 8 * j : 64 * i + 8 * j + 8, :] for i in range(8)], axis=0
        )
        back = mm(t_first, stacked(part))
        for i in range(8):
            add_rows(slice(64 * i + 8 * j, 64 * i + 8 * j + 8), back[8 * i : 8 * i + 8])
    backward = three_terms(jnp.concatenate([kron(r + 3, s + 3) for r, s in pairs], axis=0))

    for copy in first_round:
        copy.wait()
    group_in = recv_g[...]
    arrived = jnp.concatenate([recv_e[0], recv_e[1], group_in.T[0:64]], axis=1)
    hi, lo = split(arrived)
    mortar = own[...] + halves(mm(jnp.concatenate([hi, lo], axis=0), pick2[...], NT))
    hi, lo = split(mortar)
    mortar2 = jnp.concatenate([hi, lo], axis=0)
    answers = halves(mm(mortar2, pick2[...]))
    coarse_sum = group_in[0:16]
    for i in range(1, GROUP):
        coarse_sum = coarse_sum + group_in[16 * i : 16 * i + 16]
    send_e2[0, 0:64, :] = answers[:, 0:128]
    send_e2[1, 0:64, :] = answers[:, 128:256]
    send_e2[0, 64:80, :] = coarse_sum
    send_e2[1, 64:80, :] = coarse_sum
    send_g2[...] = jnp.concatenate([answers[:, 256:384], jnp.zeros((64, 128), F32)], axis=0).T
    second_round = edge_copies(send_e2, recv_e2, se2_sem, re2_sem)
    second_round += group_copies(send_g2, recv_g2, sg2_sem, rg2_sem, CAP_C)
    for copy in second_round:
        copy.start()
    recv_g2[mine, :] = send_g2[mine, :]

    picked[...] = halves(mm(mortar2, pick[0:M_DEV, :]))

    for copy in second_round:
        copy.wait()
    returned = jnp.concatenate([recv_e2[0, 0:64, :], recv_e2[1, 0:64, :], recv_g2[...].T[0:64]], axis=1)
    hi, lo = split(returned)
    returned2 = jnp.concatenate([hi, lo], axis=0)
    before = recv_e2[0, 64:80, :]
    after = recv_e2[1, 64:80, :]

    def widen(mid, left, right):
        near = jnp.where(
            iota((8, 128), 0) < 4, pltpu.roll(left, 4, 0), pltpu.roll(right, 4, 0)
        )
        return jnp.where(iota((8, 128), 1) >= 64, mid + near, 0.0)

    totals = widen(coarse_sum[0:8], before[0:8], after[0:8])
    counts = widen(coarse_sum[8:16], before[8:16], after[8:16])
    coarse = totals / (1.0 + counts)
    coarse_hi = coarse.astype(BF16).astype(F32)
    coarse2 = jnp.concatenate([coarse_hi, coarse - coarse_hi], axis=0).astype(BF16)
    spread = mm(coarse2, corner_hot[...])
    spread = spread[0:8] + spread[8:16]

    for f in range(6):
        span = slice(f * 256, (f + 1) * 256)
        value = picked[:, span] + halves(mm(returned2, pick[M_DEV:COLS, span]))
        level = jnp.concatenate([lvl[2 * f : 2 * f + 1, :], lvl[2 * f + 1 : 2 * f + 2, :]], axis=1)
        level = jnp.broadcast_to(level, (64, E_DEV))
        every = mm(backward, stacked(value))
        chosen = value
        for n in range(4):
            chosen = jnp.where(level == n + 1, every[64 * n : 64 * n + 64], chosen)
        if f < 2:
            add_rows(slice(448 * f, 448 * f + 64), chosen)
        elif f < 4:
            for i in range(8):
                first = 64 * i + 56 * (f - 2)
                add_rows(slice(first, first + 8), chosen[8 * i : 8 * i + 8])
        else:
            add_rows(pl.ds(7 * (f - 4), 64, stride=8), chosen)
    for corner in range(8):
        row = 7 * (64 * (corner // 4) + 8 * (corner // 2 % 2) + corner % 2)
        here = eight == high[corner : corner + 1, :]
        fix = jnp.where(here, spread[:, corner * 256 : (corner + 1) * 256], 0.0)
        add_rows(slice(row, row + 1), jnp.sum(fix, axis=0, keepdims=True))
    out[:, 0:128] = acc[0]
    out[:, 128:256] = acc[1]


def on_device(n_elem, nodal, metric, derivative, interp, face_level, face_target, slot_mortar, vertex_ids):
    mats = jnp.concatenate([interp, derivative[None]], axis=0)
    mats = jnp.concatenate([mats, mats.transpose(0, 2, 1)], axis=0).reshape(48, 8)
    first = jnp.broadcast_to(mats[:, None, :, None], (48, 3, 8, 8)).reshape(48, 192)
    second = jnp.broadcast_to(mats[:, None, None, :], (48, 3, 8, 8)).reshape(48, 192)
    anywhere = pl.BlockSpec(memory_space=pl.ANY)
    dma = pltpu.SemaphoreType.DMA
    return pl.pallas_call(
        functools.partial(kernel, n_elem),
        out_shape=jax.ShapeDtypeStruct((NODES, E_DEV), F32),
        in_specs=[anywhere] * 8,
        out_specs=pl.BlockSpec(memory_space=pltpu.VMEM),
        scratch_shapes=[
            pltpu.VMEM((2, NODES, 128), F32),
            pltpu.VMEM((3, NODES, E_DEV), BF16),
            pltpu.VMEM((48, 192), F32),
            pltpu.VMEM((48, 192), F32),
            pltpu.VMEM((12, 128), jnp.int32),
            pltpu.VMEM((12, 128), jnp.int32),
            pltpu.VMEM((3, 128), jnp.int32),
            pltpu.VMEM((8, E_DEV), jnp.int32),
            pltpu.VMEM((COLS, FACES), BF16),
            pltpu.VMEM((M_DEV, SLOTS), BF16),
            pltpu.VMEM((128, 8 * E_DEV), BF16),
            pltpu.VMEM((128, FACES), BF16),
            pltpu.VMEM((64, M_DEV), F32),
            pltpu.VMEM((64, FACES), F32),
            pltpu.VMEM((NODES, E_DEV), F32),
            pltpu.VMEM((2, NODES, 128), F32),
            pltpu.VMEM((2, 64, 128), F32),
            pltpu.VMEM((128, 128), F32),
            pltpu.VMEM((2, 64, 128), F32),
            pltpu.VMEM((128, 128), F32),
            pltpu.VMEM((2, 80, 128), F32),
            pltpu.VMEM((128, 128), F32),
            pltpu.VMEM((2, 80, 128), F32),
            pltpu.VMEM((128, 128), F32),
            dma((9,)),
            dma((2,)),
            dma((2,)),
            dma((7,)),
            dma((7,)),
            dma((2,)),
            dma((2,)),
            dma((7,)),
            dma((7,)),
        ],
        compiler_params=pltpu.CompilerParams(
            collective_id=0, has_side_effects=True, vmem_limit_bytes=48 * 1024 * 1024
        ),
    )(
        nodal,
        metric,
        first,
        second,
        face_level.reshape(12, 128),
        face_target.reshape(12, 128),
        slot_mortar.reshape(3, 128),
        vertex_ids,
    )


def solution(mesh):
    in_specs = (
        P(None, ("elem", "clus")),
        P(None, None, ("elem", "clus")),
        P(),
        P(),
        P(("elem", "clus")),
        P(("elem", "clus")),
        P(("elem", "clus")),
        P(None, ("elem", "clus")),
    )
    return jax.shard_map(
        functools.partial(on_device, mesh.shape["elem"]),
        mesh=mesh,
        in_specs=in_specs,
        out_specs=P(None, ("elem", "clus")),
        check_vma=False,
    )
```

```python
import functools

import jax
import jax.numpy as jnp
from jax import lax
from jax.experimental import pallas as pl
from jax.experimental.pallas import tpu as pltpu
from jax.sharding import PartitionSpec as P

CAP_E = 128
CAP_C = 16
GROUP = 8
M_DEV = 512
SLOTS = 2 * CAP_E + GROUP * CAP_C
COLS = M_DEV + SLOTS
NV_DEV = 256
E_DEV = 256
FACES = 6 * E_DEV
NODES = 512
MESH = pl.DeviceIdType.MESH
F32 = jnp.float32
BF16 = jnp.bfloat16

NT = (((1,), (1,)), ((), ()))
NN = (((1,), (0,)), ((), ()))


def mm(a, b, dims=NN):
    return lax.dot_general(a, b, dims, preferred_element_type=F32)


def split(x):
    hi = x.astype(BF16)
    return hi, (x - hi.astype(F32)).astype(BF16)


def stacked(x):
    hi, lo = split(x)
    return jnp.concatenate([hi, lo, hi], axis=0)


def halves(x):
    return x[:64] + x[64:]


def iota(shape, axis):
    return lax.broadcasted_iota(jnp.int32, shape, axis)


def three_terms(full):
    hi = full.astype(BF16).astype(F32)
    lane = iota(full.shape, 1)
    return jnp.where(lane < 128, hi, full - hi).astype(BF16)


def kernel(
    n_elem,
    u_hbm,
    met_hbm,
    deriv_hbm,
    interp_hbm,
    lvl_hbm,
    tgt_hbm,
    slot_hbm,
    vid_hbm,
    out,
    u,
    met,
    deriv,
    interp,
    small,
    ma,
    mb,
    lvl,
    tgt,
    slot,
    vid,
    pick,
    pick2,
    corner_hot,
    proj,
    own,
    picked,
    grad0,
    acc,
    send_e,
    send_g,
    recv_e,
    recv_g,
    send_e2,
    send_g2,
    recv_e2,
    recv_g2,
    in_sem,
    se_sem,
    re_sem,
    sg_sem,
    rg_sem,
    se2_sem,
    re2_sem,
    sg2_sem,
    rg2_sem,
):
    e = lax.axis_index("elem")
    c = lax.axis_index("clus")
    nxt = lax.rem(e + 1, n_elem)
    prv = lax.rem(e + n_elem - 1, n_elem)

    barrier = pltpu.get_barrier_semaphore()
    for peer in (nxt, prv):
        pl.semaphore_signal(barrier, inc=1, device_id={"elem": peer}, device_id_type=MESH)
    for k in range(1, GROUP):
        peer = lax.rem(c + k, GROUP)
        pl.semaphore_signal(barrier, inc=1, device_id={"clus": peer}, device_id_type=MESH)

    loads = [
        pltpu.make_async_copy(src, dst, in_sem.at[n])
        for n, (src, dst) in enumerate(
            [
                (tgt_hbm, tgt),
                (u_hbm.at[:, 0:128], u.at[0]),
                (u_hbm.at[:, 128:256], u.at[1]),
                (interp_hbm, interp),
                (deriv_hbm, deriv),
                (lvl_hbm, lvl),
                (vid_hbm, vid),
                (slot_hbm, slot),
                (met_hbm, met),
            ]
        )
    ]
    for load in loads:
        load.start()

    def node_rows(ref, place):
        return jnp.concatenate([ref[0, place, :], ref[1, place, :]], axis=1)

    def add_rows(place, value):
        for side in range(2):
            acc[side, place, :] = acc[side, place, :] + value[:, 128 * side : 128 * side + 128]

    def fill_pick(first, last):
        rows = iota((last - first, 128), 0) + first
        for b in range(FACES // 128):
            hot = jnp.where(rows == tgt[b : b + 1, :], 1.0, 0.0).astype(BF16)
            pick[first:last, b * 128 : (b + 1) * 128] = hot

    small[...] = jnp.zeros_like(small)
    loads[0].wait()
    fill_pick(M_DEV, COLS)

    loads[3].wait()
    loads[4].wait()
    small[0:8, 0:8] = interp[0]
    small[8:16, 0:8] = interp[1]
    small[16:24, 0:8] = deriv[...]
    lane = iota((128, 384), 1)
    inner = jnp.where(lane < 192, (lane & 63) >> 3, lane & 7)

    def widened(x, which):
        spread = jnp.where(iota((128, 384), 0) == inner + 8 * which, 1.0, 0.0)
        return jnp.dot(x, spread, precision=lax.Precision.HIGHEST, preferred_element_type=F32)

    wide = widened(small[0:24, :], 0)
    ma[0:24, :] = wide[:, 0:192]
    mb[0:24, :] = wide[:, 192:384]

    def kron(first, second):
        return jnp.concatenate(
            [
                jnp.broadcast_to(ma[8 * first + x : 8 * first + x + 1, :], (8, 192))
                * mb[8 * second : 8 * second + 8, :]
                for x in range(8)
            ],
            axis=0,
        )

    def first_kron(which):
        full = jnp.concatenate(
            [
                jnp.broadcast_to(ma[8 * which + x : 8 * which + x + 1, :], (8, 192))
                for x in range(8)
            ],
            axis=0,
        )
        keep = (iota((64, 192), 0) & 7) == (iota((64, 192), 1) & 7)
        return jnp.where(keep, full, 0.0)

    def second_kron(which):
        full = jnp.concatenate([mb[8 * which : 8 * which + 8, :]] * 8, axis=0)
        keep = (iota((64, 192), 0) >> 3) == ((iota((64, 192), 1) & 63) >> 3)
        return jnp.where(keep, full, 0.0)

    pairs = [(0, 0), (0, 1), (1, 0), (1, 1)]
    forth = three_terms(jnp.concatenate([kron(r, s) for r, s in pairs], axis=0))

    loads[1].wait()
    loads[2].wait()
    loads[5].wait()
    for f in range(6):
        if f == 0:
            trace = node_rows(u, slice(0, 64))
        elif f == 1:
            trace = node_rows(u, slice(448, 512))
        elif f == 2:
            trace = jnp.concatenate([node_rows(u, slice(64 * i, 64 * i + 8)) for i in range(8)], axis=0)
        elif f == 3:
            trace = jnp.concatenate(
                [node_rows(u, slice(64 * i + 56, 64 * i + 64)) for i in range(8)], axis=0
            )
        else:
            first = 0 if f == 4 else 7
            trace = node_rows(u, pl.ds(first, 64, stride=8))
        level = jnp.concatenate([lvl[2 * f : 2 * f + 1, :], lvl[2 * f + 1 : 2 * f + 2, :]], axis=1)
        level = jnp.broadcast_to(level, (64, E_DEV))
        every = mm(forth, stacked(trace))
        chosen = trace
        for n in range(4):
            chosen = jnp.where(level == n + 1, every[64 * n : 64 * n + 64], chosen)
        hi, lo = split(chosen)
        proj[0:64, f * 256 : (f + 1) * 256] = hi
        proj[64:128, f * 256 : (f + 1) * 256] = lo

    loads[6].wait()
    away = vid[...] - e * NV_DEV
    total_vertices = n_elem * NV_DEV
    window = jnp.where(away < 0, away + total_vertices, away)
    high = window >> 6
    low = window & 63
    sums = jnp.zeros((32, 128), F32)
    eight = iota((8, E_DEV), 0)
    lanes_rows = iota((128, E_DEV), 0) - 64
    for corner in range(8):
        row = 7 * (64 * (corner // 4) + 8 * (corner // 2 % 2) + corner % 2)
        value = jnp.broadcast_to(node_rows(u, slice(row, row + 1)), (8, E_DEV))
        hi = value.astype(BF16).astype(F32)
        here = eight == high[corner : corner + 1, :]
        parts = [
            jnp.where(here, hi, 0.0),
            jnp.where(here, value - hi, 0.0),
            jnp.where(here, 1.0, 0.0),
            jnp.zeros((8, E_DEV), F32),
        ]
        hot = jnp.where(lanes_rows == low[corner : corner + 1, :], 1.0, 0.0).astype(BF16)
        corner_hot[:, corner * 256 : (corner + 1) * 256] = hot
        sums = sums + mm(jnp.concatenate(parts, axis=0).astype(BF16), hot, NT)
    local = jnp.concatenate([sums[0:8] + sums[8:16], sums[16:24]], axis=0)

    leaving = halves(mm(proj[...], pick[M_DEV:COLS, :], NT))
    send_e[0] = leaving[:, 0:128]
    send_e[1] = leaving[:, 128:256]
    turned = jnp.concatenate([leaving[:, 256:384], jnp.zeros((64, 128), F32)], axis=0).T
    send_g[...] = turned + jnp.concatenate([local] * GROUP, axis=0)

    def edge_copies(src, dst, ssem, rsem):
        return [
            pltpu.make_async_remote_copy(
                src.at[way],
                dst.at[1 - way],
                ssem.at[way],
                rsem.at[1 - way],
                device_id={"elem": peer},
                device_id_type=MESH,
            )
            for way, peer in ((0, prv), (1, nxt))
        ]

    def group_copies(src, dst, ssem, rsem, rows):
        copies = []
        for k in range(1, GROUP):
            peer = lax.rem(c + k, GROUP)
            copies.append(
                pltpu.make_async_remote_copy(
                    src.at[pl.ds(pl.multiple_of(peer * rows, rows), rows), :],
                    dst.at[pl.ds(pl.multiple_of(c * rows, rows), rows), :],
                    ssem.at[k - 1],
                    rsem.at[k - 1],
                    device_id={"clus": peer},
                    device_id_type=MESH,
                )
            )
        return copies

    pl.semaphore_wait(barrier, GROUP + 1)
    first_round = edge_copies(send_e, recv_e, se_sem, re_sem)
    first_round += group_copies(send_g, recv_g, sg_sem, rg_sem, CAP_C)
    for copy in first_round:
        copy.start()
    mine = pl.ds(pl.multiple_of(c * CAP_C, CAP_C), CAP_C)
    recv_g[mine, :] = send_g[mine, :]

    fill_pick(0, M_DEV)
    own[...] = halves(mm(proj[...], pick[0:M_DEV, :], NT))
    loads[7].wait()
    rows2 = iota((M_DEV, 128), 0)
    for b in range(SLOTS // 128):
        hot = jnp.where(rows2 == slot[b : b + 1, :], 1.0, 0.0).astype(BF16)
        pick2[:, b * 128 : (b + 1) * 128] = hot

    turned_small = small[...].T[0:8]
    for which in range(3):
        wide = widened(turned_small, which)
        ma[24 + 8 * which : 32 + 8 * which, :] = wide[:, 0:192]
        mb[24 + 8 * which : 32 + 8 * which, :] = wide[:, 192:384]
    backward = three_terms(jnp.concatenate([kron(r + 3, s + 3) for r, s in pairs], axis=0))

    for copy in first_round:
        copy.wait()
    group_in = recv_g[...]
    arrived = jnp.concatenate([recv_e[0], recv_e[1], group_in.T[0:64]], axis=1)
    hi, lo = split(arrived)
    mortar = own[...] + halves(mm(jnp.concatenate([hi, lo], axis=0), pick2[...], NT))
    hi, lo = split(mortar)
    mortar2 = jnp.concatenate([hi, lo], axis=0)
    answers = halves(mm(mortar2, pick2[...]))
    coarse_sum = group_in[0:16]
    for i in range(1, GROUP):
        coarse_sum = coarse_sum + group_in[16 * i : 16 * i + 16]
    send_e2[0, 0:64, :] = answers[:, 0:128]
    send_e2[1, 0:64, :] = answers[:, 128:256]
    send_e2[0, 64:80, :] = coarse_sum
    send_e2[1, 64:80, :] = coarse_sum
    shifted = pltpu.roll(answers[:, 256:384], 120, 1)
    turned = jnp.concatenate([answers[:, 256:384], shifted], axis=0).T
    for i in range(GROUP):
        send_g2[8 * i : 8 * i + 8, :] = turned[16 * i : 16 * i + 8, :]
    second_round = edge_copies(send_e2, recv_e2, se2_sem, re2_sem)
    second_round += group_copies(send_g2, recv_g2, sg2_sem, rg2_sem, CAP_C // 2)
    for copy in second_round:
        copy.start()
    mine2 = pl.ds(pl.multiple_of(c * 8, 8), 8)
    recv_g2[mine2, :] = send_g2[mine2, :]

    picked[...] = halves(mm(mortar2, pick[0:M_DEV, :]))

    loads[8].wait()
    d_first = first_kron(2)
    d_second = second_kron(2)
    fore12 = three_terms(jnp.concatenate([d_first, d_second], axis=0))
    fore0 = fore12[0:64]
    t_first = three_terms(first_kron(5))
    t_second = three_terms(second_kron(5))
    for j in range(8):
        part = jnp.concatenate(
            [node_rows(u, slice(64 * i + 8 * j, 64 * i + 8 * j + 8)) for i in range(8)], axis=0
        )
        grad = mm(fore0, stacked(part))
        for i in range(8):
            grad0[64 * i + 8 * j : 64 * i + 8 * j + 8, :] = grad[8 * i : 8 * i + 8]
    for i in range(8):
        block = slice(64 * i, 64 * i + 64)
        grad = mm(fore12, stacked(node_rows(u, block)))
        flow1 = met[1, block, :].astype(F32) * grad[0:64]
        flow2 = met[2, block, :].astype(F32) * grad[64:128]
        grad0[block, :] = met[0, block, :].astype(F32) * grad0[block, :]
        back = mm(t_first, stacked(flow1)) + mm(t_second, stacked(flow2))
        acc[0, block, :] = back[:, 0:128]
        acc[1, block, :] = back[:, 128:256]
    for j in range(8):
        part = jnp.concatenate(
            [grad0[64 * i + 8 * j : 64 * i + 8 * j + 8, :] for i in range(8)], axis=0
        )
        back = mm(t_first, stacked(part))
        for i in range(8):
            add_rows(slice(64 * i + 8 * j, 64 * i + 8 * j + 8), back[8 * i : 8 * i + 8])

    for copy in second_round:
        copy.wait()
    turned = jnp.concatenate(
        [recv_g2[8 * (i // 2) : 8 * (i // 2) + 8, :] for i in range(2 * GROUP)], axis=0
    ).T
    odd = (iota((64, 128), 1) & 8) != 0
    from_group = jnp.where(odd, turned[64:128], turned[0:64])
    returned = jnp.concatenate([recv_e2[0, 0:64, :], recv_e2[1, 0:64, :], from_group], axis=1)
    hi, lo = split(returned)
    returned2 = jnp.concatenate([hi, lo], axis=0)
    before = recv_e2[0, 64:80, :]
    after = recv_e2[1, 64:80, :]

    def widen(mid, left, right):
        near = jnp.where(
            iota((8, 128), 0) < 4, pltpu.roll(left, 4, 0), pltpu.roll(right, 4, 0)
        )
        return jnp.where(iota((8, 128), 1) >= 64, mid + near, 0.0)

    totals = widen(coarse_sum[0:8], before[0:8], after[0:8])
    counts = widen(coarse_sum[8:16], before[8:16], after[8:16])
    coarse = totals / (1.0 + counts)
    coarse_hi = coarse.astype(BF16).astype(F32)
    coarse2 = jnp.concatenate([coarse_hi, coarse - coarse_hi], axis=0).astype(BF16)
    spread = mm(coarse2, corner_hot[...])
    spread = spread[0:8] + spread[8:16]

    for f in range(6):
        span = slice(f * 256, (f + 1) * 256)
        value = picked[:, span] + halves(mm(returned2, pick[M_DEV:COLS, span]))
        level = jnp.concatenate([lvl[2 * f : 2 * f + 1, :], lvl[2 * f + 1 : 2 * f + 2, :]], axis=1)
        level = jnp.broadcast_to(level, (64, E_DEV))
        every = mm(backward, stacked(value))
        chosen = value
        for n in range(4):
            chosen = jnp.where(level == n + 1, every[64 * n : 64 * n + 64], chosen)
        if f < 2:
            add_rows(slice(448 * f, 448 * f + 64), chosen)
        elif f < 4:
            for i in range(8):
                first = 64 * i + 56 * (f - 2)
                add_rows(slice(first, first + 8), chosen[8 * i : 8 * i + 8])
        else:
            add_rows(pl.ds(7 * (f - 4), 64, stride=8), chosen)
    for corner in range(8):
        row = 7 * (64 * (corner // 4) + 8 * (corner // 2 % 2) + corner % 2)
        here = eight == high[corner : corner + 1, :]
        fix = jnp.where(here, spread[:, corner * 256 : (corner + 1) * 256], 0.0)
        add_rows(slice(row, row + 1), jnp.sum(fix, axis=0, keepdims=True))
    out[:, 0:128] = acc[0]
    out[:, 128:256] = acc[1]


def on_device(n_elem, nodal, metric, derivative, interp, face_level, face_target, slot_mortar, vertex_ids):
    anywhere = pl.BlockSpec(memory_space=pltpu.HBM)
    dma = pltpu.SemaphoreType.DMA
    return pl.pallas_call(
        functools.partial(kernel, n_elem),
        out_shape=jax.ShapeDtypeStruct((NODES, E_DEV), F32),
        in_specs=[anywhere] * 8,
        out_specs=pl.BlockSpec(memory_space=pltpu.VMEM),
        scratch_shapes=[
            pltpu.VMEM((2, NODES, 128), F32),
            pltpu.VMEM((3, NODES, E_DEV), BF16),
            pltpu.VMEM((8, 8), F32),
            pltpu.VMEM((2, 8, 8), F32),
            pltpu.VMEM((128, 128), F32),
            pltpu.VMEM((48, 192), F32),
            pltpu.VMEM((48, 192), F32),
            pltpu.VMEM((12, 128), jnp.int32),
            pltpu.VMEM((12, 128), jnp.int32),
            pltpu.VMEM((3, 128), jnp.int32),
            pltpu.VMEM((8, E_DEV), jnp.int32),
            pltpu.VMEM((COLS, FACES), BF16),
            pltpu.VMEM((M_DEV, SLOTS), BF16),
            pltpu.VMEM((128, 8 * E_DEV), BF16),
            pltpu.VMEM((128, FACES), BF16),
            pltpu.VMEM((64, M_DEV), F32),
            pltpu.VMEM((64, FACES), F32),
            pltpu.VMEM((NODES, E_DEV), F32),
            pltpu.VMEM((2, NODES, 128), F32),
            pltpu.VMEM((2, 64, 128), F32),
            pltpu.VMEM((128, 128), F32),
            pltpu.VMEM((2, 64, 128), F32),
            pltpu.VMEM((128, 128), F32),
            pltpu.VMEM((2, 80, 128), F32),
            pltpu.VMEM((64, 128), F32),
            pltpu.VMEM((2, 80, 128), F32),
            pltpu.VMEM((64, 128), F32),
            dma((9,)),
            dma((2,)),
            dma((2,)),
            dma((7,)),
            dma((7,)),
            dma((2,)),
            dma((2,)),
            dma((7,)),
            dma((7,)),
        ],
        compiler_params=pltpu.CompilerParams(
            collective_id=0, has_side_effects=True, vmem_limit_bytes=48 * 1024 * 1024
        ),
    )(
        *[
            pltpu.with_memory_space_constraint(x, pltpu.HBM)
            for x in (
                nodal,
                metric,
                derivative,
                interp,
                face_level.reshape(12, 128),
                face_target.reshape(12, 128),
                slot_mortar.reshape(3, 128),
                vertex_ids,
            )
        ]
    )


def solution(mesh):
    in_specs = (
        P(None, ("elem", "clus")),
        P(None, None, ("elem", "clus")),
        P(),
        P(),
        P(("elem", "clus")),
        P(("elem", "clus")),
        P(("elem", "clus")),
        P(None, ("elem", "clus")),
    )
    return jax.shard_map(
        functools.partial(on_device, mesh.shape["elem"]),
        mesh=mesh,
        in_specs=in_specs,
        out_specs=P(None, ("elem", "clus")),
        check_vma=False,
    )
```

```python
import functools

import jax
import jax.numpy as jnp
from jax import lax
from jax.experimental import pallas as pl
from jax.experimental.pallas import tpu as pltpu
from jax.sharding import PartitionSpec as P

CAP_E = 128
CAP_C = 16
GROUP = 8
M_DEV = 512
SLOTS = 2 * CAP_E + GROUP * CAP_C
COLS = M_DEV + SLOTS
GROUP_COL = M_DEV + 2 * CAP_E
NV_DEV = 256
E_DEV = 256
FACES = 6 * E_DEV
NODES = 512
MESH = pl.DeviceIdType.MESH
F32 = jnp.float32
BF16 = jnp.bfloat16

NT = (((1,), (1,)), ((), ()))
NN = (((1,), (0,)), ((), ()))


def mm(a, b, dims=NN):
    return lax.dot_general(a, b, dims, preferred_element_type=F32)


def split(x):
    hi = x.astype(BF16)
    return hi, (x - hi.astype(F32)).astype(BF16)


def stacked(x):
    hi, lo = split(x)
    return jnp.concatenate([hi, lo, hi], axis=0)


def halves(x):
    return x[:64] + x[64:]


def two_terms(x):
    hi, lo = split(x)
    return jnp.concatenate([hi, lo], axis=0)


def iota(shape, axis):
    return lax.broadcasted_iota(jnp.int32, shape, axis)


def three_terms(full):
    hi = full.astype(BF16).astype(F32)
    lane = iota(full.shape, 1)
    return jnp.where(lane < 128, hi, full - hi).astype(BF16)


def kernel(
    n_elem,
    u_hbm,
    met_hbm,
    deriv_hbm,
    interp_hbm,
    lvl_hbm,
    tgt_hbm,
    slot_hbm,
    vid_hbm,
    out,
    u,
    met,
    deriv,
    interp,
    small,
    ma,
    mb,
    lvl,
    tgt,
    slot,
    vid,
    pick,
    pick2,
    corner_hot,
    proj,
    own,
    faces,
    answers,
    arrived,
    same,
    grad0,
    acc,
    send_e,
    send_g,
    recv_e,
    recv_g,
    send_e2,
    send_g2,
    recv_e2,
    recv_g2,
    in_sem,
    se_sem,
    re_sem,
    sg_sem,
    rg_sem,
    se2_sem,
    re2_sem,
    sg2_sem,
    rg2_sem,
):
    e = lax.axis_index("elem")
    c = lax.axis_index("clus")
    nxt = lax.rem(e + 1, n_elem)
    prv = lax.rem(e + n_elem - 1, n_elem)

    loads = [
        pltpu.make_async_copy(src, dst, in_sem.at[n])
        for n, (src, dst) in enumerate(
            [
                (tgt_hbm, tgt),
                (u_hbm.at[:, 0:128], u.at[0]),
                (u_hbm.at[:, 128:256], u.at[1]),
                (interp_hbm, interp),
                (deriv_hbm, deriv),
                (lvl_hbm, lvl),
                (vid_hbm, vid),
                (slot_hbm, slot),
                (met_hbm, met),
            ]
        )
    ]
    for load in loads[:8]:
        load.start()

    barrier = pltpu.get_barrier_semaphore()
    for peer in (nxt, prv):
        pl.semaphore_signal(barrier, inc=1, device_id={"elem": peer}, device_id_type=MESH)
    for k in range(1, GROUP):
        peer = lax.rem(c + k, GROUP)
        pl.semaphore_signal(barrier, inc=1, device_id={"clus": peer}, device_id_type=MESH)

    def node_rows(ref, place):
        return jnp.concatenate([ref[0, place, :], ref[1, place, :]], axis=1)

    def add_rows(place, value):
        for side in range(2):
            acc[side, place, :] = acc[side, place, :] + value[:, 128 * side : 128 * side + 128]

    def fill_pick(first, last):
        rows = iota((last - first, 128), 0) + first
        for b in range(FACES // 128):
            hot = jnp.where(rows == tgt[b : b + 1, :], 1.0, 0.0).astype(BF16)
            pick[first:last, b * 128 : (b + 1) * 128] = hot

    small[...] = jnp.zeros_like(small)
    loads[0].wait()
    fill_pick(M_DEV, COLS)

    loads[3].wait()
    loads[4].wait()
    small[0:8, 0:8] = interp[0]
    small[8:16, 0:8] = interp[1]
    small[16:24, 0:8] = deriv[...]
    lane = iota((128, 384), 1)
    inner = jnp.where(lane < 192, (lane & 63) >> 3, lane & 7)

    def widened(x, which):
        spread = jnp.where(iota((128, 384), 0) == inner + 8 * which, 1.0, 0.0)
        return jnp.dot(x, spread, precision=lax.Precision.HIGHEST, preferred_element_type=F32)

    wide = widened(small[0:24, :], 0)
    ma[0:24, :] = wide[:, 0:192]
    mb[0:24, :] = wide[:, 192:384]

    def kron(first, second):
        return jnp.concatenate(
            [
                jnp.broadcast_to(ma[8 * first + x : 8 * first + x + 1, :], (8, 192))
                * mb[8 * second : 8 * second + 8, :]
                for x in range(8)
            ],
            axis=0,
        )

    def first_kron(which):
        full = jnp.concatenate(
            [
                jnp.broadcast_to(ma[8 * which + x : 8 * which + x + 1, :], (8, 192))
                for x in range(8)
            ],
            axis=0,
        )
        keep = (iota((64, 192), 0) & 7) == (iota((64, 192), 1) & 7)
        return jnp.where(keep, full, 0.0)

    def second_kron(which):
        full = jnp.concatenate([mb[8 * which : 8 * which + 8, :]] * 8, axis=0)
        keep = (iota((64, 192), 0) >> 3) == ((iota((64, 192), 1) & 63) >> 3)
        return jnp.where(keep, full, 0.0)

    pairs = [(0, 0), (0, 1), (1, 0), (1, 1)]
    forth = three_terms(jnp.concatenate([kron(r, s) for r, s in pairs], axis=0))

    loads[1].wait()
    loads[2].wait()
    loads[8].start()
    loads[5].wait()
    def across(ref, first, count):
        row = jnp.concatenate([ref[n : n + 1, :] for n in range(first, first + count)], axis=1)
        return jnp.broadcast_to(row, (64, 128 * count))

    def by_level(level, mats, value):
        every = mm(mats, stacked(value))
        chosen = value
        for n in range(4):
            chosen = jnp.where(level == n + 1, every[64 * n : 64 * n + 64], chosen)
        return chosen

    far = [slice(8 * j, 8 * j + 8) for j in range(64)]
    trace = jnp.concatenate(
        [
            node_rows(u, slice(0, 64)),
            node_rows(u, slice(448, 512)),
            jnp.concatenate([node_rows(u, far[8 * i]) for i in range(8)], axis=0),
            jnp.concatenate([node_rows(u, far[8 * i + 7]) for i in range(8)], axis=0),
            node_rows(u, pl.ds(0, 64, stride=8)),
            node_rows(u, pl.ds(7, 64, stride=8)),
        ],
        axis=1,
    )
    hi, lo = split(by_level(across(lvl, 0, 12), forth, trace))
    proj[0:64, :] = hi
    proj[64:128, :] = lo

    loads[6].wait()
    away = vid[...] - e * NV_DEV
    total_vertices = n_elem * NV_DEV
    window = jnp.where(away < 0, away + total_vertices, away)
    high = window >> 6
    low = window & 63
    sums = jnp.zeros((32, 128), F32)
    eight = iota((8, E_DEV), 0)
    lanes_rows = iota((128, E_DEV), 0) - 64
    for corner in range(8):
        row = 7 * (64 * (corner // 4) + 8 * (corner // 2 % 2) + corner % 2)
        value = jnp.broadcast_to(node_rows(u, slice(row, row + 1)), (8, E_DEV))
        hi = value.astype(BF16).astype(F32)
        here = eight == high[corner : corner + 1, :]
        parts = [
            jnp.where(here, hi, 0.0),
            jnp.where(here, value - hi, 0.0),
            jnp.where(here, 1.0, 0.0),
            jnp.zeros((8, E_DEV), F32),
        ]
        hot = jnp.where(lanes_rows == low[corner : corner + 1, :], 1.0, 0.0).astype(BF16)
        corner_hot[:, corner * 256 : (corner + 1) * 256] = hot
        sums = sums + mm(jnp.concatenate(parts, axis=0).astype(BF16), hot, NT)
    local = jnp.concatenate([sums[0:8] + sums[8:16], sums[16:24]], axis=0)

    leaving = halves(mm(proj[...], pick[GROUP_COL:COLS, :], NT))
    turned = jnp.concatenate([leaving, jnp.zeros((64, 128), F32)], axis=0).T
    send_g[...] = turned + jnp.concatenate([local] * GROUP, axis=0)

    def edge_copies(src, dst, ssem, rsem):
        return [
            pltpu.make_async_remote_copy(
                src.at[way],
                dst.at[1 - way],
                ssem.at[way],
                rsem.at[1 - way],
                device_id={"elem": peer},
                device_id_type=MESH,
            )
            for way, peer in ((0, prv), (1, nxt))
        ]

    def group_copies(src, dst, ssem, rsem, rows):
        copies = []
        for k in range(1, GROUP):
            peer = lax.rem(c + k, GROUP)
            copies.append(
                pltpu.make_async_remote_copy(
                    src.at[pl.ds(pl.multiple_of(peer * rows, rows), rows), :],
                    dst.at[pl.ds(pl.multiple_of(c * rows, rows), rows), :],
                    ssem.at[k - 1],
                    rsem.at[k - 1],
                    device_id={"clus": peer},
                    device_id_type=MESH,
                )
            )
        return copies

    pl.semaphore_wait(barrier, GROUP + 1)
    group_round = group_copies(send_g, recv_g, sg_sem, rg_sem, CAP_C)
    for copy in group_round:
        copy.start()
    leaving = halves(mm(proj[...], pick[M_DEV:GROUP_COL, :], NT))
    send_e[0] = leaving[:, 0:128]
    send_e[1] = leaving[:, 128:256]
    edge_round = edge_copies(send_e, recv_e, se_sem, re_sem)
    for copy in edge_round:
        copy.start()
    mine = pl.ds(pl.multiple_of(c * CAP_C, CAP_C), CAP_C)
    recv_g[mine, :] = send_g[mine, :]

    fill_pick(0, M_DEV)
    own[...] = halves(mm(proj[...], pick[0:M_DEV, :], NT))
    loads[7].wait()
    rows2 = iota((M_DEV, 128), 0)
    for b in range(SLOTS // 128):
        hot = jnp.where(rows2 == slot[b : b + 1, :], 1.0, 0.0).astype(BF16)
        pick2[:, b * 128 : (b + 1) * 128] = hot

    turned_small = small[...].T[0:8]
    for which in range(3):
        wide = widened(turned_small, which)
        ma[24 + 8 * which : 32 + 8 * which, :] = wide[:, 0:192]
        mb[24 + 8 * which : 32 + 8 * which, :] = wide[:, 192:384]
    backward = three_terms(jnp.concatenate([kron(r + 3, s + 3) for r, s in pairs], axis=0))

    level_row = jnp.concatenate([lvl[n : n + 1, :] for n in range(12)], axis=1)
    level_row = jnp.broadcast_to(level_row, (16, FACES)).astype(F32).astype(BF16)
    slot_level = mm(level_row, pick[M_DEV:COLS, :], NT)[0:1]
    slot_level = jnp.broadcast_to(slot_level, (64, SLOTS))

    slot_row = jnp.concatenate([slot[b : b + 1, :] for b in range(3)], axis=1)
    for b in range(3):
        column = jnp.broadcast_to(slot[b : b + 1, :], (128, 128)).T
        column = jnp.concatenate([column] * 3, axis=1)
        same[128 * b : 128 * b + 128, :] = jnp.where(column == slot_row, 1.0, 0.0).astype(BF16)

    answers[...] = halves(mm(two_terms(own[...]), pick2[...]))
    for copy in edge_round:
        copy.wait()
    arrived[:, 0:256] = two_terms(jnp.concatenate([recv_e[0], recv_e[1]], axis=1))
    answers[...] = answers[...] + halves(mm(arrived[:, 0:256], same[0:256, :]))
    for copy in group_round:
        copy.wait()
    group_in = recv_g[...]
    from_group = two_terms(group_in.T[0:64])
    arrived[:, 256:384] = from_group
    answer = answers[:, 256:384] + halves(mm(from_group, same[256:384, 256:384]))
    shifted = pltpu.roll(answer, 120, 1)
    turned = jnp.concatenate([answer, shifted], axis=0).T
    for i in range(GROUP):
        send_g2[8 * i : 8 * i + 8, :] = turned[16 * i : 16 * i + 8, :]
    group_round = group_copies(send_g2, recv_g2, sg2_sem, rg2_sem, CAP_C // 2)
    for copy in group_round:
        copy.start()
    answer = answers[:, 0:256] + halves(mm(from_group, same[256:384, 0:256]))
    coarse_sum = group_in[0:16]
    for i in range(1, GROUP):
        coarse_sum = coarse_sum + group_in[16 * i : 16 * i + 16]
    send_e2[0, 0:64, :] = answer[:, 0:128]
    send_e2[1, 0:64, :] = answer[:, 128:256]
    send_e2[0, 64:80, :] = coarse_sum
    send_e2[1, 64:80, :] = coarse_sum
    edge_round = edge_copies(send_e2, recv_e2, se2_sem, re2_sem)
    for copy in edge_round:
        copy.start()
    mine2 = pl.ds(pl.multiple_of(c * 8, 8), 8)
    recv_g2[mine2, :] = send_g2[mine2, :]

    loads[8].wait()
    d_first = first_kron(2)
    d_second = second_kron(2)
    fore12 = three_terms(jnp.concatenate([d_first, d_second], axis=0))
    fore0 = fore12[0:64]
    t_first = three_terms(first_kron(5))
    t_second = three_terms(second_kron(5))
    for j in range(8):
        part = jnp.concatenate(
            [node_rows(u, slice(64 * i + 8 * j, 64 * i + 8 * j + 8)) for i in range(8)], axis=0
        )
        grad = mm(fore0, stacked(part))
        for i in range(8):
            grad0[64 * i + 8 * j : 64 * i + 8 * j + 8, :] = grad[8 * i : 8 * i + 8]
    for i in range(8):
        block = slice(64 * i, 64 * i + 64)
        grad = mm(fore12, stacked(node_rows(u, block)))
        flow1 = met[1, block, :].astype(F32) * grad[0:64]
        flow2 = met[2, block, :].astype(F32) * grad[64:128]
        grad0[block, :] = met[0, block, :].astype(F32) * grad0[block, :]
        back = mm(t_first, stacked(flow1)) + mm(t_second, stacked(flow2))
        acc[0, block, :] = back[:, 0:128]
        acc[1, block, :] = back[:, 128:256]
    for j in range(8):
        part = jnp.concatenate(
            [grad0[64 * i + 8 * j : 64 * i + 8 * j + 8, :] for i in range(8)], axis=0
        )
        back = mm(t_first, stacked(part))
        for i in range(8):
            add_rows(slice(64 * i + 8 * j, 64 * i + 8 * j + 8), back[8 * i : 8 * i + 8])

    mortar = own[...] + halves(mm(arrived[...], pick2[...], NT))
    picked = halves(mm(two_terms(mortar), pick[0:M_DEV, :]))
    faces[...] = by_level(across(lvl, 0, 12), backward, picked)

    for copy in edge_round:
        copy.wait()
    value = jnp.concatenate([recv_e2[0, 0:64, :], recv_e2[1, 0:64, :]], axis=1)
    value = two_terms(by_level(slot_level[:, 0:256], backward, value))
    faces[...] = faces[...] + halves(mm(value, pick[M_DEV:GROUP_COL, :]))
    before = recv_e2[0, 64:80, :]
    after = recv_e2[1, 64:80, :]

    def widen(mid, left, right):
        near = jnp.where(
            iota((8, 128), 0) < 4, pltpu.roll(left, 4, 0), pltpu.roll(right, 4, 0)
        )
        return jnp.where(iota((8, 128), 1) >= 64, mid + near, 0.0)

    totals = widen(coarse_sum[0:8], before[0:8], after[0:8])
    counts = widen(coarse_sum[8:16], before[8:16], after[8:16])
    coarse = totals / (1.0 + counts)
    coarse_hi = coarse.astype(BF16).astype(F32)
    coarse2 = jnp.concatenate([coarse_hi, coarse - coarse_hi], axis=0).astype(BF16)
    spread = mm(coarse2, corner_hot[...])
    spread = spread[0:8] + spread[8:16]

    for corner in range(8):
        row = 7 * (64 * (corner // 4) + 8 * (corner // 2 % 2) + corner % 2)
        here = eight == high[corner : corner + 1, :]
        fix = jnp.where(here, spread[:, corner * 256 : (corner + 1) * 256], 0.0)
        add_rows(slice(row, row + 1), jnp.sum(fix, axis=0, keepdims=True))
    for copy in group_round:
        copy.wait()
    turned = jnp.concatenate(
        [recv_g2[8 * (i // 2) : 8 * (i // 2) + 8, :] for i in range(2 * GROUP)], axis=0
    ).T
    odd = (iota((64, 128), 1) & 8) != 0
    value = jnp.where(odd, turned[64:128], turned[0:64])
    value = two_terms(by_level(slot_level[:, 256:384], backward, value))
    total = faces[...] + halves(mm(value, pick[GROUP_COL:COLS, :]))
    add_rows(pl.ds(0, 64, stride=8), total[:, 1024:1280])
    add_rows(pl.ds(7, 64, stride=8), total[:, 1280:1536])
    for i in range(8):
        block = node_rows(acc, slice(64 * i, 64 * i + 64))
        if i == 0:
            block = block + total[:, 0:256]
        if i == 7:
            block = block + total[:, 256:512]
        near = block[0:8] + total[8 * i : 8 * i + 8, 512:768]
        away = block[56:64] + total[8 * i : 8 * i + 8, 768:1024]
        out[64 * i : 64 * i + 64, :] = jnp.concatenate([near, block[8:56], away], axis=0)


def on_device(n_elem, nodal, metric, derivative, interp, face_level, face_target, slot_mortar, vertex_ids):
    anywhere = pl.BlockSpec(memory_space=pltpu.HBM)
    dma = pltpu.SemaphoreType.DMA
    return pl.pallas_call(
        functools.partial(kernel, n_elem),
        out_shape=jax.ShapeDtypeStruct((NODES, E_DEV), F32),
        in_specs=[anywhere] * 8,
        out_specs=pl.BlockSpec(memory_space=pltpu.VMEM),
        scratch_shapes=[
            pltpu.VMEM((2, NODES, 128), F32),
            pltpu.VMEM((3, NODES, E_DEV), BF16),
            pltpu.VMEM((8, 8), F32),
            pltpu.VMEM((2, 8, 8), F32),
            pltpu.VMEM((128, 128), F32),
            pltpu.VMEM((48, 192), F32),
            pltpu.VMEM((48, 192), F32),
            pltpu.VMEM((12, 128), jnp.int32),
            pltpu.VMEM((12, 128), jnp.int32),
            pltpu.VMEM((3, 128), jnp.int32),
            pltpu.VMEM((8, E_DEV), jnp.int32),
            pltpu.VMEM((COLS, FACES), BF16),
            pltpu.VMEM((M_DEV, SLOTS), BF16),
            pltpu.VMEM((128, 8 * E_DEV), BF16),
            pltpu.VMEM((128, FACES), BF16),
            pltpu.VMEM((64, M_DEV), F32),
            pltpu.VMEM((64, FACES), F32),
            pltpu.VMEM((64, SLOTS), F32),
            pltpu.VMEM((128, SLOTS), BF16),
            pltpu.VMEM((SLOTS, SLOTS), BF16),
            pltpu.VMEM((NODES, E_DEV), F32),
            pltpu.VMEM((2, NODES, 128), F32),
            pltpu.VMEM((2, 64, 128), F32),
            pltpu.VMEM((128, 128), F32),
            pltpu.VMEM((2, 64, 128), F32),
            pltpu.VMEM((128, 128), F32),
            pltpu.VMEM((2, 80, 128), F32),
            pltpu.VMEM((64, 128), F32),
            pltpu.VMEM((2, 80, 128), F32),
            pltpu.VMEM((64, 128), F32),
            dma((9,)),
            dma((2,)),
            dma((2,)),
            dma((7,)),
            dma((7,)),
            dma((2,)),
            dma((2,)),
            dma((7,)),
            dma((7,)),
        ],
        compiler_params=pltpu.CompilerParams(
            collective_id=0, has_side_effects=True, vmem_limit_bytes=48 * 1024 * 1024
        ),
    )(
        *[
            pltpu.with_memory_space_constraint(x, pltpu.HBM)
            for x in (
                nodal,
                metric,
                derivative,
                interp,
                face_level.reshape(12, 128),
                face_target.reshape(12, 128),
                slot_mortar.reshape(3, 128),
                vertex_ids,
            )
        ]
    )


def solution(mesh):
    in_specs = (
        P(None, ("elem", "clus")),
        P(None, None, ("elem", "clus")),
        P(),
        P(),
        P(("elem", "clus")),
        P(("elem", "clus")),
        P(("elem", "clus")),
        P(None, ("elem", "clus")),
    )
    return jax.shard_map(
        functools.partial(on_device, mesh.shape["elem"]),
        mesh=mesh,
        in_specs=in_specs,
        out_specs=P(None, ("elem", "clus")),
        check_vma=False,
    )
```

```python
import functools

import jax
import jax.numpy as jnp
from jax import lax
from jax.experimental import pallas as pl
from jax.experimental.pallas import tpu as pltpu
from jax.sharding import PartitionSpec as P

CAP_E = 128
CAP_C = 16
GROUP = 8
M_DEV = 512
SLOTS = 2 * CAP_E + GROUP * CAP_C
COLS = M_DEV + SLOTS
GROUP_COL = M_DEV + 2 * CAP_E
NV_DEV = 256
E_DEV = 256
FACES = 6 * E_DEV
NODES = 512
MESH = pl.DeviceIdType.MESH
F32 = jnp.float32
BF16 = jnp.bfloat16

NT = (((1,), (1,)), ((), ()))
NN = (((1,), (0,)), ((), ()))


def mm(a, b, dims=NN):
    return lax.dot_general(a, b, dims, preferred_element_type=F32)


def split(x):
    hi = x.astype(BF16)
    return hi, (x - hi.astype(F32)).astype(BF16)


def stacked(x):
    hi, lo = split(x)
    return jnp.concatenate([hi, lo, hi], axis=0)


def halves(x):
    return x[:64] + x[64:]


def two_terms(x):
    hi, lo = split(x)
    return jnp.concatenate([hi, lo], axis=0)


def iota(shape, axis):
    return lax.broadcasted_iota(jnp.int32, shape, axis)


def three_terms(full):
    hi = full.astype(BF16).astype(F32)
    lane = iota(full.shape, 1)
    return jnp.where(lane < 128, hi, full - hi).astype(BF16)


def kernel(
    n_elem,
    u_hbm,
    met_hbm,
    deriv_hbm,
    interp_hbm,
    lvl_hbm,
    tgt_hbm,
    slot_hbm,
    vid_hbm,
    out,
    u,
    met,
    deriv,
    interp,
    small,
    ma,
    mb,
    lvl,
    tgt,
    slot,
    vid,
    pick,
    pick2,
    corner_hot,
    proj,
    own,
    faces,
    answers,
    arrived,
    same,
    grad0,
    acc,
    send_e,
    send_g,
    recv_e,
    recv_g,
    send_e2,
    send_g2,
    recv_e2,
    recv_g2,
    send_c,
    recv_c,
    in_sem,
    se_sem,
    re_sem,
    sg_sem,
    rg_sem,
    se2_sem,
    re2_sem,
    sg2_sem,
    rg2_sem,
    sc_sem,
    rc_sem,
):
    e = lax.axis_index("elem")
    c = lax.axis_index("clus")
    nxt = lax.rem(e + 1, n_elem)
    prv = lax.rem(e + n_elem - 1, n_elem)

    loads = [
        pltpu.make_async_copy(src, dst, in_sem.at[n])
        for n, (src, dst) in enumerate(
            [
                (tgt_hbm, tgt),
                (u_hbm.at[:, 0:128], u.at[0]),
                (u_hbm.at[:, 128:256], u.at[1]),
                (interp_hbm, interp),
                (deriv_hbm, deriv),
                (lvl_hbm, lvl),
                (vid_hbm, vid),
                (slot_hbm, slot),
                (met_hbm, met),
            ]
        )
    ]
    for load in loads[:8]:
        load.start()

    barrier = pltpu.get_barrier_semaphore()
    for peer in (nxt, prv):
        pl.semaphore_signal(barrier, inc=1, device_id={"elem": peer}, device_id_type=MESH)
    for k in range(1, GROUP):
        peer = lax.rem(c + k, GROUP)
        pl.semaphore_signal(barrier, inc=1, device_id={"clus": peer}, device_id_type=MESH)

    def node_rows(ref, place):
        return jnp.concatenate([ref[0, place, :], ref[1, place, :]], axis=1)

    def add_rows(place, value):
        for side in range(2):
            acc[side, place, :] = acc[side, place, :] + value[:, 128 * side : 128 * side + 128]

    def fill_pick(first, last):
        rows = iota((last - first, 128), 0) + first
        for b in range(FACES // 128):
            hot = jnp.where(rows == tgt[b : b + 1, :], 1.0, 0.0).astype(BF16)
            pick[first:last, b * 128 : (b + 1) * 128] = hot

    small[...] = jnp.zeros_like(small)
    for load in loads[:7]:
        load.wait()
    loads[8].start()
    fill_pick(M_DEV, COLS)

    small[0:8, 0:8] = interp[0]
    small[8:16, 0:8] = interp[1]
    small[16:24, 0:8] = deriv[...]
    lane = iota((128, 384), 1)
    inner = jnp.where(lane < 192, (lane & 63) >> 3, lane & 7)

    def widened(x, which):
        spread = jnp.where(iota((128, 384), 0) == inner + 8 * which, 1.0, 0.0)
        return jnp.dot(x, spread, precision=lax.Precision.HIGHEST, preferred_element_type=F32)

    wide = widened(small[0:24, :], 0)
    ma[0:24, :] = wide[:, 0:192]
    mb[0:24, :] = wide[:, 192:384]

    def kron(first, second):
        return jnp.concatenate(
            [
                jnp.broadcast_to(ma[8 * first + x : 8 * first + x + 1, :], (8, 192))
                * mb[8 * second : 8 * second + 8, :]
                for x in range(8)
            ],
            axis=0,
        )

    def first_kron(which):
        full = jnp.concatenate(
            [
                jnp.broadcast_to(ma[8 * which + x : 8 * which + x + 1, :], (8, 192))
                for x in range(8)
            ],
            axis=0,
        )
        keep = (iota((64, 192), 0) & 7) == (iota((64, 192), 1) & 7)
        return jnp.where(keep, full, 0.0)

    def second_kron(which):
        full = jnp.concatenate([mb[8 * which : 8 * which + 8, :]] * 8, axis=0)
        keep = (iota((64, 192), 0) >> 3) == ((iota((64, 192), 1) & 63) >> 3)
        return jnp.where(keep, full, 0.0)

    pairs = [(0, 0), (0, 1), (1, 0), (1, 1)]
    forth = three_terms(jnp.concatenate([kron(r, s) for r, s in pairs], axis=0))

    def across(ref, first, count):
        row = jnp.concatenate([ref[n : n + 1, :] for n in range(first, first + count)], axis=1)
        return jnp.broadcast_to(row, (64, 128 * count))

    def by_level(level, mats, value):
        every = mm(mats, stacked(value))
        chosen = value
        for n in range(4):
            chosen = jnp.where(level == n + 1, every[64 * n : 64 * n + 64], chosen)
        return chosen

    far = [slice(8 * j, 8 * j + 8) for j in range(64)]
    trace = jnp.concatenate(
        [
            node_rows(u, slice(0, 64)),
            node_rows(u, slice(448, 512)),
            jnp.concatenate([node_rows(u, far[8 * i]) for i in range(8)], axis=0),
            jnp.concatenate([node_rows(u, far[8 * i + 7]) for i in range(8)], axis=0),
            node_rows(u, pl.ds(0, 64, stride=8)),
            node_rows(u, pl.ds(7, 64, stride=8)),
        ],
        axis=1,
    )
    hi, lo = split(by_level(across(lvl, 0, 12), forth, trace))
    proj[0:64, :] = hi
    proj[64:128, :] = lo

    away = vid[...] - e * NV_DEV
    total_vertices = n_elem * NV_DEV
    window = jnp.where(away < 0, away + total_vertices, away)
    high = window >> 6
    low = window & 63
    sums = jnp.zeros((32, 128), F32)
    eight = iota((8, E_DEV), 0)
    lanes_rows = iota((128, E_DEV), 0) - 64
    for corner in range(8):
        row = 7 * (64 * (corner // 4) + 8 * (corner // 2 % 2) + corner % 2)
        value = jnp.broadcast_to(node_rows(u, slice(row, row + 1)), (8, E_DEV))
        hi = value.astype(BF16).astype(F32)
        here = eight == high[corner : corner + 1, :]
        parts = [
            jnp.where(here, hi, 0.0),
            jnp.where(here, value - hi, 0.0),
            jnp.where(here, 1.0, 0.0),
            jnp.zeros((8, E_DEV), F32),
        ]
        hot = jnp.where(lanes_rows == low[corner : corner + 1, :], 1.0, 0.0).astype(BF16)
        corner_hot[:, corner * 256 : (corner + 1) * 256] = hot
        sums = sums + mm(jnp.concatenate(parts, axis=0).astype(BF16), hot, NT)
    local = jnp.concatenate([sums[0:8] + sums[8:16], sums[16:24]], axis=0)

    leaving = halves(mm(proj[...], pick[M_DEV:COLS, :], NT))
    send_e[0] = leaving[:, 0:128]
    send_e[1] = leaving[:, 128:256]
    turned = jnp.concatenate([leaving[:, 256:384], jnp.zeros((64, 128), F32)], axis=0).T
    send_g[...] = turned + jnp.concatenate([local] * GROUP, axis=0)

    def edge_copies(src, dst, ssem, rsem):
        return [
            pltpu.make_async_remote_copy(
                src.at[way],
                dst.at[1 - way],
                ssem.at[way],
                rsem.at[1 - way],
                device_id={"elem": peer},
                device_id_type=MESH,
            )
            for way, peer in ((0, prv), (1, nxt))
        ]

    def group_copies(src, dst, ssem, rsem, rows):
        copies = []
        for k in (4, 5, 3, 2, 6, 7, 1):
            peer = lax.rem(c + k, GROUP)
            copies.append(
                pltpu.make_async_remote_copy(
                    src.at[pl.ds(pl.multiple_of(peer * rows, rows), rows), :],
                    dst.at[pl.ds(pl.multiple_of(c * rows, rows), rows), :],
                    ssem.at[k - 1],
                    rsem.at[k - 1],
                    device_id={"clus": peer},
                    device_id_type=MESH,
                )
            )
        return copies

    pl.semaphore_wait(barrier, GROUP + 1)
    edge_round = edge_copies(send_e, recv_e, se_sem, re_sem)
    group_round = group_copies(send_g, recv_g, sg_sem, rg_sem, CAP_C)
    for copy in edge_round + group_round:
        copy.start()
    mine = pl.ds(pl.multiple_of(c * CAP_C, CAP_C), CAP_C)
    recv_g[mine, :] = send_g[mine, :]

    fill_pick(0, M_DEV)
    own[...] = halves(mm(proj[...], pick[0:M_DEV, :], NT))
    loads[7].wait()
    rows2 = iota((M_DEV, 128), 0)
    for b in range(SLOTS // 128):
        hot = jnp.where(rows2 == slot[b : b + 1, :], 1.0, 0.0).astype(BF16)
        pick2[:, b * 128 : (b + 1) * 128] = hot

    turned_small = small[...].T[0:8]
    for which in range(3):
        wide = widened(turned_small, which)
        ma[24 + 8 * which : 32 + 8 * which, :] = wide[:, 0:192]
        mb[24 + 8 * which : 32 + 8 * which, :] = wide[:, 192:384]
    backward = three_terms(jnp.concatenate([kron(r + 3, s + 3) for r, s in pairs], axis=0))

    level_row = jnp.concatenate([lvl[n : n + 1, :] for n in range(12)], axis=1)
    level_row = jnp.broadcast_to(level_row, (16, FACES)).astype(F32).astype(BF16)
    slot_level = mm(level_row, pick[M_DEV:COLS, :], NT)[0:1]
    slot_level = jnp.broadcast_to(slot_level, (64, SLOTS))

    slot_row = jnp.concatenate([slot[b : b + 1, :] for b in range(3)], axis=1)
    for b in range(3):
        column = jnp.broadcast_to(slot[b : b + 1, :], (128, 128)).T
        column = jnp.concatenate([column] * 3, axis=1)
        same[128 * b : 128 * b + 128, :] = jnp.where(column == slot_row, 1.0, 0.0).astype(BF16)

    answers[...] = halves(mm(two_terms(own[...]), pick2[...]))
    for copy in group_round:
        copy.wait()
    group_in = recv_g[...]
    coarse_sum = group_in[0:16]
    for i in range(1, GROUP):
        coarse_sum = coarse_sum + group_in[16 * i : 16 * i + 16]
    send_c[0] = coarse_sum
    send_c[1] = coarse_sum
    coarse_round = edge_copies(send_c, recv_c, sc_sem, rc_sem)
    for copy in coarse_round:
        copy.start()
    from_group = two_terms(group_in.T[0:64])
    arrived[:, 256:384] = from_group
    answers[...] = answers[...] + halves(mm(from_group, same[256:384, :]))
    for copy in edge_round:
        copy.wait()
    from_edge = two_terms(jnp.concatenate([recv_e[0], recv_e[1]], axis=1))
    arrived[:, 0:256] = from_edge
    answer = answers[...] + halves(mm(from_edge, same[0:256, :]))
    send_e2[0] = answer[:, 0:128]
    send_e2[1] = answer[:, 128:256]
    edge_round = edge_copies(send_e2, recv_e2, se2_sem, re2_sem)
    for copy in edge_round:
        copy.start()
    shifted = pltpu.roll(answer[:, 256:384], 120, 1)
    turned = jnp.concatenate([answer[:, 256:384], shifted], axis=0).T
    for i in range(GROUP):
        send_g2[8 * i : 8 * i + 8, :] = turned[16 * i : 16 * i + 8, :]
    group_round = group_copies(send_g2, recv_g2, sg2_sem, rg2_sem, CAP_C // 2)
    for copy in group_round:
        copy.start()
    mine2 = pl.ds(pl.multiple_of(c * 8, 8), 8)
    recv_g2[mine2, :] = send_g2[mine2, :]

    loads[8].wait()
    d_first = first_kron(2)
    d_second = second_kron(2)
    fore12 = three_terms(jnp.concatenate([d_first, d_second], axis=0))
    fore0 = fore12[0:64]
    t_first = three_terms(first_kron(5))
    t_second = three_terms(second_kron(5))
    for j in range(8):
        part = jnp.concatenate(
            [node_rows(u, slice(64 * i + 8 * j, 64 * i + 8 * j + 8)) for i in range(8)], axis=0
        )
        grad = mm(fore0, stacked(part))
        for i in range(8):
            grad0[64 * i + 8 * j : 64 * i + 8 * j + 8, :] = grad[8 * i : 8 * i + 8]
    for i in range(8):
        block = slice(64 * i, 64 * i + 64)
        grad = mm(fore12, stacked(node_rows(u, block)))
        flow1 = met[1, block, :].astype(F32) * grad[0:64]
        flow2 = met[2, block, :].astype(F32) * grad[64:128]
        grad0[block, :] = met[0, block, :].astype(F32) * grad0[block, :]
        back = mm(t_first, stacked(flow1)) + mm(t_second, stacked(flow2))
        acc[0, block, :] = back[:, 0:128]
        acc[1, block, :] = back[:, 128:256]
    for j in range(8):
        part = jnp.concatenate(
            [grad0[64 * i + 8 * j : 64 * i + 8 * j + 8, :] for i in range(8)], axis=0
        )
        back = mm(t_first, stacked(part))
        for i in range(8):
            add_rows(slice(64 * i + 8 * j, 64 * i + 8 * j + 8), back[8 * i : 8 * i + 8])

    mortar = own[...] + halves(mm(arrived[...], pick2[...], NT))
    picked = halves(mm(two_terms(mortar), pick[0:M_DEV, :]))
    faces[...] = by_level(across(lvl, 0, 12), backward, picked)

    for copy in coarse_round:
        copy.wait()
    before = recv_c[0]
    after = recv_c[1]

    def widen(mid, left, right):
        near = jnp.where(
            iota((8, 128), 0) < 4, pltpu.roll(left, 4, 0), pltpu.roll(right, 4, 0)
        )
        return jnp.where(iota((8, 128), 1) >= 64, mid + near, 0.0)

    totals = widen(coarse_sum[0:8], before[0:8], after[0:8])
    counts = widen(coarse_sum[8:16], before[8:16], after[8:16])
    coarse = totals / (1.0 + counts)
    coarse_hi = coarse.astype(BF16).astype(F32)
    coarse2 = jnp.concatenate([coarse_hi, coarse - coarse_hi], axis=0).astype(BF16)
    spread = mm(coarse2, corner_hot[...])
    spread = spread[0:8] + spread[8:16]

    for corner in range(8):
        row = 7 * (64 * (corner // 4) + 8 * (corner // 2 % 2) + corner % 2)
        here = eight == high[corner : corner + 1, :]
        fix = jnp.where(here, spread[:, corner * 256 : (corner + 1) * 256], 0.0)
        add_rows(slice(row, row + 1), jnp.sum(fix, axis=0, keepdims=True))
    for copy in group_round:
        copy.wait()
    turned = jnp.concatenate(
        [recv_g2[8 * (i // 2) : 8 * (i // 2) + 8, :] for i in range(2 * GROUP)], axis=0
    ).T
    odd = (iota((64, 128), 1) & 8) != 0
    value = jnp.where(odd, turned[64:128], turned[0:64])
    value = two_terms(by_level(slot_level[:, 256:384], backward, value))
    faces[...] = faces[...] + halves(mm(value, pick[GROUP_COL:COLS, :]))

    for copy in edge_round:
        copy.wait()
    value = jnp.concatenate([recv_e2[0], recv_e2[1]], axis=1)
    value = two_terms(by_level(slot_level[:, 0:256], backward, value))
    total = faces[...] + halves(mm(value, pick[M_DEV:GROUP_COL, :]))
    add_rows(pl.ds(0, 64, stride=8), total[:, 1024:1280])
    add_rows(pl.ds(7, 64, stride=8), total[:, 1280:1536])
    for i in range(8):
        block = node_rows(acc, slice(64 * i, 64 * i + 64))
        if i == 0:
            block = block + total[:, 0:256]
        if i == 7:
            block = block + total[:, 256:512]
        near = block[0:8] + total[8 * i : 8 * i + 8, 512:768]
        away = block[56:64] + total[8 * i : 8 * i + 8, 768:1024]
        out[64 * i : 64 * i + 64, :] = jnp.concatenate([near, block[8:56], away], axis=0)


def on_device(n_elem, nodal, metric, derivative, interp, face_level, face_target, slot_mortar, vertex_ids):
    anywhere = pl.BlockSpec(memory_space=pltpu.HBM)
    dma = pltpu.SemaphoreType.DMA
    return pl.pallas_call(
        functools.partial(kernel, n_elem),
        out_shape=jax.ShapeDtypeStruct((NODES, E_DEV), F32),
        in_specs=[anywhere] * 8,
        out_specs=pl.BlockSpec(memory_space=pltpu.VMEM),
        scratch_shapes=[
            pltpu.VMEM((2, NODES, 128), F32),
            pltpu.VMEM((3, NODES, E_DEV), BF16),
            pltpu.VMEM((8, 8), F32),
            pltpu.VMEM((2, 8, 8), F32),
            pltpu.VMEM((128, 128), F32),
            pltpu.VMEM((48, 192), F32),
            pltpu.VMEM((48, 192), F32),
            pltpu.VMEM((12, 128), jnp.int32),
            pltpu.VMEM((12, 128), jnp.int32),
            pltpu.VMEM((3, 128), jnp.int32),
            pltpu.VMEM((8, E_DEV), jnp.int32),
            pltpu.VMEM((COLS, FACES), BF16),
            pltpu.VMEM((M_DEV, SLOTS), BF16),
            pltpu.VMEM((128, 8 * E_DEV), BF16),
            pltpu.VMEM((128, FACES), BF16),
            pltpu.VMEM((64, M_DEV), F32),
            pltpu.VMEM((64, FACES), F32),
            pltpu.VMEM((64, SLOTS), F32),
            pltpu.VMEM((128, SLOTS), BF16),
            pltpu.VMEM((SLOTS, SLOTS), BF16),
            pltpu.VMEM((NODES, E_DEV), F32),
            pltpu.VMEM((2, NODES, 128), F32),
            pltpu.VMEM((2, 64, 128), F32),
            pltpu.VMEM((128, 128), F32),
            pltpu.VMEM((2, 64, 128), F32),
            pltpu.VMEM((128, 128), F32),
            pltpu.VMEM((2, 64, 128), F32),
            pltpu.VMEM((64, 128), F32),
            pltpu.VMEM((2, 64, 128), F32),
            pltpu.VMEM((64, 128), F32),
            pltpu.VMEM((2, 16, 128), F32),
            pltpu.VMEM((2, 16, 128), F32),
            dma((9,)),
            dma((2,)),
            dma((2,)),
            dma((7,)),
            dma((7,)),
            dma((2,)),
            dma((2,)),
            dma((7,)),
            dma((7,)),
            dma((2,)),
            dma((2,)),
        ],
        compiler_params=pltpu.CompilerParams(
            collective_id=0, has_side_effects=True, vmem_limit_bytes=48 * 1024 * 1024
        ),
    )(
        *[
            pltpu.with_memory_space_constraint(x, pltpu.HBM)
            for x in (
                nodal,
                metric,
                derivative,
                interp,
                face_level.reshape(12, 128),
                face_target.reshape(12, 128),
                slot_mortar.reshape(3, 128),
                vertex_ids,
            )
        ]
    )


def solution(mesh):
    in_specs = (
        P(None, ("elem", "clus")),
        P(None, None, ("elem", "clus")),
        P(),
        P(),
        P(("elem", "clus")),
        P(("elem", "clus")),
        P(("elem", "clus")),
        P(None, ("elem", "clus")),
    )
    return jax.shard_map(
        functools.partial(on_device, mesh.shape["elem"]),
        mesh=mesh,
        in_specs=in_specs,
        out_specs=P(None, ("elem", "clus")),
        check_vma=False,
    )
```

```python
import functools

import jax
import jax.numpy as jnp
from jax import lax
from jax.experimental import pallas as pl
from jax.experimental.pallas import tpu as pltpu
from jax.sharding import PartitionSpec as P

CAP_E = 128
CAP_C = 16
GROUP = 8
M_DEV = 512
SLOTS = 2 * CAP_E + GROUP * CAP_C
COLS = M_DEV + SLOTS
GROUP_COL = M_DEV + 2 * CAP_E
NV_DEV = 256
E_DEV = 256
FACES = 6 * E_DEV
NODES = 512
MESH = pl.DeviceIdType.MESH
F32 = jnp.float32
BF16 = jnp.bfloat16

NT = (((1,), (1,)), ((), ()))
NN = (((1,), (0,)), ((), ()))


def mm(a, b, dims=NN):
    return lax.dot_general(a, b, dims, preferred_element_type=F32)


def split(x):
    hi = x.astype(BF16)
    return hi, (x - hi.astype(F32)).astype(BF16)


def stacked(x):
    hi, lo = split(x)
    return jnp.concatenate([hi, lo, hi], axis=0)


def halves(x):
    return x[:64] + x[64:]


def two_terms(x):
    hi, lo = split(x)
    return jnp.concatenate([hi, lo], axis=0)


def iota(shape, axis):
    return lax.broadcasted_iota(jnp.int32, shape, axis)


def three_terms(full):
    hi = full.astype(BF16).astype(F32)
    lane = iota(full.shape, 1)
    return jnp.where(lane < 128, hi, full - hi).astype(BF16)


def kernel(
    n_elem,
    u_hbm,
    met_hbm,
    deriv_hbm,
    interp_hbm,
    lvl_hbm,
    tgt_hbm,
    slot_hbm,
    vid_hbm,
    out,
    u,
    met,
    deriv,
    interp,
    small,
    ma,
    mb,
    lvl,
    tgt,
    slot,
    vid,
    pick,
    pick2,
    corner_hot,
    terms,
    slot_level,
    own,
    faces,
    answers,
    arrived,
    returned,
    same,
    grad0,
    acc,
    send_e,
    send_g,
    recv_e,
    recv_g,
    send_e2,
    send_g2,
    recv_e2,
    recv_g2,
    send_c,
    recv_c,
    in_sem,
    se_sem,
    re_sem,
    sg_sem,
    rg_sem,
    se2_sem,
    re2_sem,
    sg2_sem,
    rg2_sem,
    sc_sem,
    rc_sem,
):
    e = lax.axis_index("elem")
    c = lax.axis_index("clus")
    nxt = lax.rem(e + 1, n_elem)
    prv = lax.rem(e + n_elem - 1, n_elem)

    loads = [
        pltpu.make_async_copy(src, dst, in_sem.at[n])
        for n, (src, dst) in enumerate(
            [
                (tgt_hbm, tgt),
                (u_hbm.at[:, 0:128], u.at[0]),
                (u_hbm.at[:, 128:256], u.at[1]),
                (interp_hbm, interp),
                (deriv_hbm, deriv),
                (lvl_hbm, lvl),
                (vid_hbm, vid),
                (slot_hbm, slot),
                (met_hbm, met),
            ]
        )
    ]
    for load in loads[:8]:
        load.start()

    barrier = pltpu.get_barrier_semaphore()
    for peer in (nxt, prv):
        pl.semaphore_signal(barrier, inc=1, device_id={"elem": peer}, device_id_type=MESH)
    for k in range(1, GROUP):
        peer = lax.rem(c + k, GROUP)
        pl.semaphore_signal(barrier, inc=1, device_id={"clus": peer}, device_id_type=MESH)

    def node_rows(ref, place):
        return jnp.concatenate([ref[0, place, :], ref[1, place, :]], axis=1)

    def add_rows(place, value):
        for side in range(2):
            acc[side, place, :] = acc[side, place, :] + value[:, 128 * side : 128 * side + 128]

    def fill_pick(first, last):
        rows = iota((last - first, 128), 0) + first
        for b in range(FACES // 128):
            hot = jnp.where(rows == tgt[b : b + 1, :], 1.0, 0.0).astype(BF16)
            pick[first:last, b * 128 : (b + 1) * 128] = hot

    small[...] = jnp.zeros_like(small)
    for load in loads[:7]:
        load.wait()
    loads[8].start()
    fill_pick(M_DEV, COLS)

    small[0:8, 0:8] = interp[0]
    small[8:16, 0:8] = interp[1]
    small[16:24, 0:8] = deriv[...]
    lane = iota((128, 384), 1)
    inner = jnp.where(lane < 192, (lane & 63) >> 3, lane & 7)

    def widened(x, which):
        spread = jnp.where(iota((128, 384), 0) == inner + 8 * which, 1.0, 0.0)
        return jnp.dot(x, spread, precision=lax.Precision.HIGHEST, preferred_element_type=F32)

    wide = widened(small[0:24, :], 0)
    ma[0:24, :] = wide[:, 0:192]
    mb[0:24, :] = wide[:, 192:384]

    def kron(first, second):
        return jnp.concatenate(
            [
                jnp.broadcast_to(ma[8 * first + x : 8 * first + x + 1, :], (8, 192))
                * mb[8 * second : 8 * second + 8, :]
                for x in range(8)
            ],
            axis=0,
        )

    def first_kron(which):
        full = jnp.concatenate(
            [
                jnp.broadcast_to(ma[8 * which + x : 8 * which + x + 1, :], (8, 192))
                for x in range(8)
            ],
            axis=0,
        )
        keep = (iota((64, 192), 0) & 7) == (iota((64, 192), 1) & 7)
        return jnp.where(keep, full, 0.0)

    def second_kron(which):
        full = jnp.concatenate([mb[8 * which : 8 * which + 8, :]] * 8, axis=0)
        keep = (iota((64, 192), 0) >> 3) == ((iota((64, 192), 1) & 63) >> 3)
        return jnp.where(keep, full, 0.0)

    pairs = [(0, 0), (0, 1), (1, 0), (1, 1)]
    forth = three_terms(jnp.concatenate([kron(r, s) for r, s in pairs], axis=0))

    def across(ref, first, count):
        row = jnp.concatenate([ref[n : n + 1, :] for n in range(first, first + count)], axis=1)
        return jnp.broadcast_to(row, (64, 128 * count))

    def by_level(level, mats, value):
        every = mm(mats, stacked(value))
        chosen = value
        for n in range(4):
            chosen = jnp.where(level == n + 1, every[64 * n : 64 * n + 64], chosen)
        return chosen

    far = [slice(8 * j, 8 * j + 8) for j in range(64)]
    def traces():
        return jnp.concatenate(
            [
                node_rows(u, slice(0, 64)),
                node_rows(u, slice(448, 512)),
                jnp.concatenate([node_rows(u, far[8 * i]) for i in range(8)], axis=0),
                jnp.concatenate([node_rows(u, far[8 * i + 7]) for i in range(8)], axis=0),
                node_rows(u, pl.ds(0, 64, stride=8)),
                node_rows(u, pl.ds(7, 64, stride=8)),
            ],
            axis=1,
        )

    terms[0:128, :] = two_terms(traces())
    terms[128:144, :] = across(lvl, 0, 12)[0:16].astype(F32).astype(BF16)

    away = vid[...] - e * NV_DEV
    total_vertices = n_elem * NV_DEV
    window = jnp.where(away < 0, away + total_vertices, away)
    high = window >> 6
    low = window & 63
    sums = jnp.zeros((32, 128), F32)
    eight = iota((8, E_DEV), 0)
    lanes_rows = iota((128, E_DEV), 0) - 64
    for corner in range(8):
        row = 7 * (64 * (corner // 4) + 8 * (corner // 2 % 2) + corner % 2)
        value = jnp.broadcast_to(node_rows(u, slice(row, row + 1)), (8, E_DEV))
        hi = value.astype(BF16).astype(F32)
        here = eight == high[corner : corner + 1, :]
        parts = [
            jnp.where(here, hi, 0.0),
            jnp.where(here, value - hi, 0.0),
            jnp.where(here, 1.0, 0.0),
            jnp.zeros((8, E_DEV), F32),
        ]
        hot = jnp.where(lanes_rows == low[corner : corner + 1, :], 1.0, 0.0).astype(BF16)
        corner_hot[:, corner * 256 : (corner + 1) * 256] = hot
        sums = sums + mm(jnp.concatenate(parts, axis=0).astype(BF16), hot, NT)
    local = jnp.concatenate([sums[0:8] + sums[8:16], sums[16:24]], axis=0)

    raw = mm(terms[...], pick[M_DEV:COLS, :], NT)
    slot_level[...] = jnp.broadcast_to(raw[128:129], (64, SLOTS))
    leaving = by_level(slot_level[...], forth, halves(raw[0:128]))
    send_e[0] = leaving[:, 0:128]
    send_e[1] = leaving[:, 128:256]
    turned = jnp.concatenate([leaving[:, 256:384], jnp.zeros((64, 128), F32)], axis=0).T
    send_g[...] = turned + jnp.concatenate([local] * GROUP, axis=0)

    def edge_copies(src, dst, ssem, rsem):
        return [
            pltpu.make_async_remote_copy(
                src.at[way],
                dst.at[1 - way],
                ssem.at[way],
                rsem.at[1 - way],
                device_id={"elem": peer},
                device_id_type=MESH,
            )
            for way, peer in ((0, prv), (1, nxt))
        ]

    def group_copies(src, dst, ssem, rsem, rows):
        copies = []
        for k in (4, 5, 3, 2, 6, 7, 1):
            peer = lax.rem(c + k, GROUP)
            copies.append(
                pltpu.make_async_remote_copy(
                    src.at[pl.ds(pl.multiple_of(peer * rows, rows), rows), :],
                    dst.at[pl.ds(pl.multiple_of(c * rows, rows), rows), :],
                    ssem.at[k - 1],
                    rsem.at[k - 1],
                    device_id={"clus": peer},
                    device_id_type=MESH,
                )
            )
        return copies

    pl.semaphore_wait(barrier, GROUP + 1)
    edge_round = edge_copies(send_e, recv_e, se_sem, re_sem)
    group_round = group_copies(send_g, recv_g, sg_sem, rg_sem, CAP_C)
    for copy in edge_round + group_round:
        copy.start()
    mine = pl.ds(pl.multiple_of(c * CAP_C, CAP_C), CAP_C)
    recv_g[mine, :] = send_g[mine, :]

    fill_pick(0, M_DEV)
    own[...] = halves(
        mm(two_terms(by_level(across(lvl, 0, 12), forth, traces())), pick[0:M_DEV, :], NT)
    )
    loads[7].wait()
    rows2 = iota((M_DEV, 128), 0)
    for b in range(SLOTS // 128):
        hot = jnp.where(rows2 == slot[b : b + 1, :], 1.0, 0.0).astype(BF16)
        pick2[:, b * 128 : (b + 1) * 128] = hot

    turned_small = small[...].T[0:8]
    for which in range(3):
        wide = widened(turned_small, which)
        ma[24 + 8 * which : 32 + 8 * which, :] = wide[:, 0:192]
        mb[24 + 8 * which : 32 + 8 * which, :] = wide[:, 192:384]
    backward = three_terms(jnp.concatenate([kron(r + 3, s + 3) for r, s in pairs], axis=0))

    slot_row = jnp.concatenate([slot[b : b + 1, :] for b in range(3)], axis=1)
    for b in range(3):
        column = jnp.broadcast_to(slot[b : b + 1, :], (128, 128)).T
        column = jnp.concatenate([column] * 3, axis=1)
        same[128 * b : 128 * b + 128, :] = jnp.where(column == slot_row, 1.0, 0.0).astype(BF16)

    answers[...] = halves(mm(two_terms(own[...]), pick2[...]))
    for copy in group_round:
        copy.wait()
    group_in = recv_g[...]
    coarse_sum = group_in[0:16]
    for i in range(1, GROUP):
        coarse_sum = coarse_sum + group_in[16 * i : 16 * i + 16]
    send_c[0] = coarse_sum
    send_c[1] = coarse_sum
    coarse_round = edge_copies(send_c, recv_c, sc_sem, rc_sem)
    for copy in coarse_round:
        copy.start()
    arrived[:, 256:384] = two_terms(group_in.T[0:64])
    for copy in edge_round:
        copy.wait()
    arrived[:, 0:256] = two_terms(jnp.concatenate([recv_e[0], recv_e[1]], axis=1))
    answer = answers[...] + halves(mm(arrived[...], same[...]))
    send_e2[0] = answer[:, 0:128]
    send_e2[1] = answer[:, 128:256]
    edge_round = edge_copies(send_e2, recv_e2, se2_sem, re2_sem)
    for copy in edge_round:
        copy.start()
    shifted = pltpu.roll(answer[:, 256:384], 120, 1)
    turned = jnp.concatenate([answer[:, 256:384], shifted], axis=0).T
    for i in range(GROUP):
        send_g2[8 * i : 8 * i + 8, :] = turned[16 * i : 16 * i + 8, :]
    group_round = group_copies(send_g2, recv_g2, sg2_sem, rg2_sem, CAP_C // 2)
    for copy in group_round:
        copy.start()
    mine2 = pl.ds(pl.multiple_of(c * 8, 8), 8)
    recv_g2[mine2, :] = send_g2[mine2, :]

    loads[8].wait()
    d_first = first_kron(2)
    d_second = second_kron(2)
    fore12 = three_terms(jnp.concatenate([d_first, d_second], axis=0))
    fore0 = fore12[0:64]
    t_first = three_terms(first_kron(5))
    t_second = three_terms(second_kron(5))
    for j in range(8):
        part = jnp.concatenate(
            [node_rows(u, slice(64 * i + 8 * j, 64 * i + 8 * j + 8)) for i in range(8)], axis=0
        )
        grad = mm(fore0, stacked(part))
        for i in range(8):
            grad0[64 * i + 8 * j : 64 * i + 8 * j + 8, :] = grad[8 * i : 8 * i + 8]
    for i in range(8):
        block = slice(64 * i, 64 * i + 64)
        grad = mm(fore12, stacked(node_rows(u, block)))
        flow1 = met[1, block, :].astype(F32) * grad[0:64]
        flow2 = met[2, block, :].astype(F32) * grad[64:128]
        grad0[block, :] = met[0, block, :].astype(F32) * grad0[block, :]
        back = mm(t_first, stacked(flow1)) + mm(t_second, stacked(flow2))
        acc[0, block, :] = back[:, 0:128]
        acc[1, block, :] = back[:, 128:256]
    for j in range(8):
        part = jnp.concatenate(
            [grad0[64 * i + 8 * j : 64 * i + 8 * j + 8, :] for i in range(8)], axis=0
        )
        back = mm(t_first, stacked(part))
        for i in range(8):
            add_rows(slice(64 * i + 8 * j, 64 * i + 8 * j + 8), back[8 * i : 8 * i + 8])

    mortar = own[...] + halves(mm(arrived[...], pick2[...], NT))
    picked = halves(mm(two_terms(mortar), pick[0:M_DEV, :]))
    faces[...] = by_level(across(lvl, 0, 12), backward, picked)

    for copy in coarse_round:
        copy.wait()
    before = recv_c[0]
    after = recv_c[1]

    def widen(mid, left, right):
        near = jnp.where(
            iota((8, 128), 0) < 4, pltpu.roll(left, 4, 0), pltpu.roll(right, 4, 0)
        )
        return jnp.where(iota((8, 128), 1) >= 64, mid + near, 0.0)

    totals = widen(coarse_sum[0:8], before[0:8], after[0:8])
    counts = widen(coarse_sum[8:16], before[8:16], after[8:16])
    coarse = totals / (1.0 + counts)
    coarse_hi = coarse.astype(BF16).astype(F32)
    coarse2 = jnp.concatenate([coarse_hi, coarse - coarse_hi], axis=0).astype(BF16)
    spread = mm(coarse2, corner_hot[...])
    spread = spread[0:8] + spread[8:16]

    for corner in range(8):
        row = 7 * (64 * (corner // 4) + 8 * (corner // 2 % 2) + corner % 2)
        here = eight == high[corner : corner + 1, :]
        fix = jnp.where(here, spread[:, corner * 256 : (corner + 1) * 256], 0.0)
        add_rows(slice(row, row + 1), jnp.sum(fix, axis=0, keepdims=True))
    for copy in group_round:
        copy.wait()
    turned = jnp.concatenate(
        [recv_g2[8 * (i // 2) : 8 * (i // 2) + 8, :] for i in range(2 * GROUP)], axis=0
    ).T
    odd = (iota((64, 128), 1) & 8) != 0
    value = jnp.where(odd, turned[64:128], turned[0:64])
    returned[:, 256:384] = two_terms(by_level(slot_level[:, 256:384], backward, value))

    for copy in edge_round:
        copy.wait()
    value = jnp.concatenate([recv_e2[0], recv_e2[1]], axis=1)
    returned[:, 0:256] = two_terms(by_level(slot_level[:, 0:256], backward, value))
    total = faces[...] + halves(mm(returned[...], pick[M_DEV:COLS, :]))
    add_rows(pl.ds(0, 64, stride=8), total[:, 1024:1280])
    add_rows(pl.ds(7, 64, stride=8), total[:, 1280:1536])
    for i in range(8):
        block = node_rows(acc, slice(64 * i, 64 * i + 64))
        if i == 0:
            block = block + total[:, 0:256]
        if i == 7:
            block = block + total[:, 256:512]
        near = block[0:8] + total[8 * i : 8 * i + 8, 512:768]
        away = block[56:64] + total[8 * i : 8 * i + 8, 768:1024]
        out[64 * i : 64 * i + 64, :] = jnp.concatenate([near, block[8:56], away], axis=0)


def on_device(n_elem, nodal, metric, derivative, interp, face_level, face_target, slot_mortar, vertex_ids):
    anywhere = pl.BlockSpec(memory_space=pltpu.HBM)
    dma = pltpu.SemaphoreType.DMA
    return pl.pallas_call(
        functools.partial(kernel, n_elem),
        out_shape=jax.ShapeDtypeStruct((NODES, E_DEV), F32),
        in_specs=[anywhere] * 8,
        out_specs=pl.BlockSpec(memory_space=pltpu.VMEM),
        scratch_shapes=[
            pltpu.VMEM((2, NODES, 128), F32),
            pltpu.VMEM((3, NODES, E_DEV), BF16),
            pltpu.VMEM((8, 8), F32),
            pltpu.VMEM((2, 8, 8), F32),
            pltpu.VMEM((128, 128), F32),
            pltpu.VMEM((48, 192), F32),
            pltpu.VMEM((48, 192), F32),
            pltpu.VMEM((12, 128), jnp.int32),
            pltpu.VMEM((12, 128), jnp.int32),
            pltpu.VMEM((3, 128), jnp.int32),
            pltpu.VMEM((8, E_DEV), jnp.int32),
            pltpu.VMEM((COLS, FACES), BF16),
            pltpu.VMEM((M_DEV, SLOTS), BF16),
            pltpu.VMEM((128, 8 * E_DEV), BF16),
            pltpu.VMEM((144, FACES), BF16),
            pltpu.VMEM((64, SLOTS), F32),
            pltpu.VMEM((64, M_DEV), F32),
            pltpu.VMEM((64, FACES), F32),
            pltpu.VMEM((64, SLOTS), F32),
            pltpu.VMEM((128, SLOTS), BF16),
            pltpu.VMEM((128, SLOTS), BF16),
            pltpu.VMEM((SLOTS, SLOTS), BF16),
            pltpu.VMEM((NODES, E_DEV), F32),
            pltpu.VMEM((2, NODES, 128), F32),
            pltpu.VMEM((2, 64, 128), F32),
            pltpu.VMEM((128, 128), F32),
            pltpu.VMEM((2, 64, 128), F32),
            pltpu.VMEM((128, 128), F32),
            pltpu.VMEM((2, 64, 128), F32),
            pltpu.VMEM((64, 128), F32),
            pltpu.VMEM((2, 64, 128), F32),
            pltpu.VMEM((64, 128), F32),
            pltpu.VMEM((2, 16, 128), F32),
            pltpu.VMEM((2, 16, 128), F32),
            dma((9,)),
            dma((2,)),
            dma((2,)),
            dma((7,)),
            dma((7,)),
            dma((2,)),
            dma((2,)),
            dma((7,)),
            dma((7,)),
            dma((2,)),
            dma((2,)),
        ],
        compiler_params=pltpu.CompilerParams(
            collective_id=0, has_side_effects=True, vmem_limit_bytes=48 * 1024 * 1024
        ),
    )(
        *[
            pltpu.with_memory_space_constraint(x, pltpu.HBM)
            for x in (
                nodal,
                metric,
                derivative,
                interp,
                face_level.reshape(12, 128),
                face_target.reshape(12, 128),
                slot_mortar.reshape(3, 128),
                vertex_ids,
            )
        ]
    )


def solution(mesh):
    in_specs = (
        P(None, ("elem", "clus")),
        P(None, None, ("elem", "clus")),
        P(),
        P(),
        P(("elem", "clus")),
        P(("elem", "clus")),
        P(("elem", "clus")),
        P(None, ("elem", "clus")),
    )
    return jax.shard_map(
        functools.partial(on_device, mesh.shape["elem"]),
        mesh=mesh,
        in_specs=in_specs,
        out_specs=P(None, ("elem", "clus")),
        check_vma=False,
    )
```

```python
import functools

import jax
import jax.numpy as jnp
from jax import lax
from jax.experimental import pallas as pl
from jax.experimental.pallas import tpu as pltpu
from jax.sharding import PartitionSpec as P

CAP_E = 128
CAP_C = 16
GROUP = 8
M_DEV = 512
SLOTS = 2 * CAP_E + GROUP * CAP_C
COLS = M_DEV + SLOTS
NV_DEV = 256
E_DEV = 256
FACES = 6 * E_DEV
NODES = 512
MESH = pl.DeviceIdType.MESH
F32 = jnp.float32
BF16 = jnp.bfloat16

NT = (((1,), (1,)), ((), ()))
NN = (((1,), (0,)), ((), ()))


def mm(a, b, dims=NN):
    return lax.dot_general(a, b, dims, preferred_element_type=F32)


def split(x):
    hi = x.astype(BF16)
    return hi, (x - hi.astype(F32)).astype(BF16)


def stacked(x):
    hi, lo = split(x)
    return jnp.concatenate([hi, lo, hi], axis=0)


def halves(x):
    return x[:64] + x[64:]


def two_terms(x):
    hi, lo = split(x)
    return jnp.concatenate([hi, lo], axis=0)


def iota(shape, axis):
    return lax.broadcasted_iota(jnp.int32, shape, axis)


def three_terms(full):
    hi = full.astype(BF16).astype(F32)
    lane = iota(full.shape, 1)
    return jnp.where(lane < 128, hi, full - hi).astype(BF16)


def kernel(
    n_elem,
    u_hbm,
    met_hbm,
    deriv_hbm,
    interp_hbm,
    lvl_hbm,
    tgt_hbm,
    slot_hbm,
    vid_hbm,
    acc,
    faces,
    returned,
    sent,
    u,
    met,
    deriv,
    interp,
    small,
    ma,
    mb,
    lvl,
    tgt,
    slot,
    vid,
    pick,
    pick2,
    corner_hot,
    terms,
    slot_level,
    own,
    answers,
    arrived,
    same,
    grad0,
    send_e,
    send_g,
    recv_e,
    recv_g,
    send_e2,
    send_g2,
    recv_e2,
    recv_g2,
    send_c,
    recv_c,
    in_sem,
    se_sem,
    re_sem,
    sg_sem,
    rg_sem,
    se2_sem,
    re2_sem,
    sg2_sem,
    rg2_sem,
    sc_sem,
    rc_sem,
):
    e = lax.axis_index("elem")
    c = lax.axis_index("clus")
    nxt = lax.rem(e + 1, n_elem)
    prv = lax.rem(e + n_elem - 1, n_elem)

    loads = [
        pltpu.make_async_copy(src, dst, in_sem.at[n])
        for n, (src, dst) in enumerate(
            [
                (tgt_hbm, tgt),
                (u_hbm.at[:, 0:128], u.at[0]),
                (u_hbm.at[:, 128:256], u.at[1]),
                (interp_hbm, interp),
                (deriv_hbm, deriv),
                (lvl_hbm, lvl),
                (vid_hbm, vid),
                (slot_hbm, slot),
                (met_hbm, met),
            ]
        )
    ]
    for load in loads[:8]:
        load.start()

    barrier = pltpu.get_barrier_semaphore()
    for peer in (nxt, prv):
        pl.semaphore_signal(barrier, inc=1, device_id={"elem": peer}, device_id_type=MESH)
    for k in range(1, GROUP):
        peer = lax.rem(c + k, GROUP)
        pl.semaphore_signal(barrier, inc=1, device_id={"clus": peer}, device_id_type=MESH)

    def node_rows(ref, place):
        return jnp.concatenate([ref[0, place, :], ref[1, place, :]], axis=1)

    def add_rows(place, value):
        for side in range(2):
            acc[side, place, :] = acc[side, place, :] + value[:, 128 * side : 128 * side + 128]

    def fill_pick(ref, first, last):
        rows = iota((last - first, 128), 0) + first
        for side in range(2):
            for f in range(6):
                row = 2 * f + side
                place = 128 * (6 * side + f)
                hot = jnp.where(rows == tgt[row : row + 1, :], 1.0, 0.0).astype(BF16)
                ref[:, place : place + 128] = hot

    small[...] = jnp.zeros_like(small)
    for load in loads[:7]:
        load.wait()
    loads[8].start()
    fill_pick(sent, M_DEV, COLS)

    small[0:8, 0:8] = interp[0]
    small[8:16, 0:8] = interp[1]
    small[16:24, 0:8] = deriv[...]
    lane = iota((128, 384), 1)
    inner = jnp.where(lane < 192, (lane & 63) >> 3, lane & 7)

    def widened(x, which):
        spread = jnp.where(iota((128, 384), 0) == inner + 8 * which, 1.0, 0.0)
        return jnp.dot(x, spread, precision=lax.Precision.HIGHEST, preferred_element_type=F32)

    wide = widened(small[0:24, :], 0)
    ma[0:24, :] = wide[:, 0:192]
    mb[0:24, :] = wide[:, 192:384]

    def kron(first, second):
        return jnp.concatenate(
            [
                jnp.broadcast_to(ma[8 * first + x : 8 * first + x + 1, :], (8, 192))
                * mb[8 * second : 8 * second + 8, :]
                for x in range(8)
            ],
            axis=0,
        )

    def first_kron(which):
        full = jnp.concatenate(
            [
                jnp.broadcast_to(ma[8 * which + x : 8 * which + x + 1, :], (8, 192))
                for x in range(8)
            ],
            axis=0,
        )
        keep = (iota((64, 192), 0) & 7) == (iota((64, 192), 1) & 7)
        return jnp.where(keep, full, 0.0)

    def second_kron(which):
        full = jnp.concatenate([mb[8 * which : 8 * which + 8, :]] * 8, axis=0)
        keep = (iota((64, 192), 0) >> 3) == ((iota((64, 192), 1) & 63) >> 3)
        return jnp.where(keep, full, 0.0)

    pairs = [(0, 0), (0, 1), (1, 0), (1, 1)]
    forth = three_terms(jnp.concatenate([kron(r, s) for r, s in pairs], axis=0))

    def across(rows):
        order = [2 * f + side for side in range(2) for f in range(6)]
        row = jnp.concatenate([lvl[n : n + 1, :] for n in order], axis=1)
        return jnp.broadcast_to(row, (rows, FACES))

    def by_level(level, mats, value):
        every = mm(mats, stacked(value))
        chosen = value
        for n in range(4):
            chosen = jnp.where(level == n + 1, every[64 * n : 64 * n + 64], chosen)
        return chosen

    far = [slice(8 * j, 8 * j + 8) for j in range(64)]
    def traces():
        parts = []
        for side in range(2):
            parts += [
                u[side, 0:64, :],
                u[side, 448:512, :],
                jnp.concatenate([u[side, far[8 * i], :] for i in range(8)], axis=0),
                jnp.concatenate([u[side, far[8 * i + 7], :] for i in range(8)], axis=0),
                u[side, pl.ds(0, 64, stride=8), :],
                u[side, pl.ds(7, 64, stride=8), :],
            ]
        return jnp.concatenate(parts, axis=1)

    terms[0:128, :] = two_terms(traces())
    terms[128:144, :] = across(16).astype(F32).astype(BF16)

    away = vid[...] - e * NV_DEV
    total_vertices = n_elem * NV_DEV
    window = jnp.where(away < 0, away + total_vertices, away)
    high = window >> 6
    low = window & 63
    sums = jnp.zeros((32, 128), F32)
    eight = iota((8, E_DEV), 0)
    lanes_rows = iota((128, E_DEV), 0) - 64
    for corner in range(8):
        row = 7 * (64 * (corner // 4) + 8 * (corner // 2 % 2) + corner % 2)
        value = jnp.broadcast_to(node_rows(u, slice(row, row + 1)), (8, E_DEV))
        hi = value.astype(BF16).astype(F32)
        here = eight == high[corner : corner + 1, :]
        parts = [
            jnp.where(here, hi, 0.0),
            jnp.where(here, value - hi, 0.0),
            jnp.where(here, 1.0, 0.0),
            jnp.zeros((8, E_DEV), F32),
        ]
        hot = jnp.where(lanes_rows == low[corner : corner + 1, :], 1.0, 0.0).astype(BF16)
        corner_hot[:, corner * 256 : (corner + 1) * 256] = hot
        sums = sums + mm(jnp.concatenate(parts, axis=0).astype(BF16), hot, NT)
    local = jnp.concatenate([sums[0:8] + sums[8:16], sums[16:24]], axis=0)

    raw = mm(terms[...], sent[...], NT)
    slot_level[...] = jnp.broadcast_to(raw[128:129], (64, SLOTS))
    leaving = by_level(slot_level[...], forth, halves(raw[0:128]))
    send_e[0] = leaving[:, 0:128]
    send_e[1] = leaving[:, 128:256]
    turned = jnp.concatenate([leaving[:, 256:384], jnp.zeros((64, 128), F32)], axis=0).T
    send_g[...] = turned + jnp.concatenate([local] * GROUP, axis=0)

    def edge_copies(src, dst, ssem, rsem):
        return [
            pltpu.make_async_remote_copy(
                src.at[way],
                dst.at[1 - way],
                ssem.at[way],
                rsem.at[1 - way],
                device_id={"elem": peer},
                device_id_type=MESH,
            )
            for way, peer in ((0, prv), (1, nxt))
        ]

    def group_copies(src, dst, ssem, rsem, rows):
        copies = []
        for k in (4, 5, 3, 2, 6, 7, 1):
            peer = lax.rem(c + k, GROUP)
            copies.append(
                pltpu.make_async_remote_copy(
                    src.at[pl.ds(pl.multiple_of(peer * rows, rows), rows), :],
                    dst.at[pl.ds(pl.multiple_of(c * rows, rows), rows), :],
                    ssem.at[k - 1],
                    rsem.at[k - 1],
                    device_id={"clus": peer},
                    device_id_type=MESH,
                )
            )
        return copies

    pl.semaphore_wait(barrier, GROUP + 1)
    edge_round = edge_copies(send_e, recv_e, se_sem, re_sem)
    group_round = group_copies(send_g, recv_g, sg_sem, rg_sem, CAP_C)
    for copy in edge_round + group_round:
        copy.start()
    mine = pl.ds(pl.multiple_of(c * CAP_C, CAP_C), CAP_C)
    recv_g[mine, :] = send_g[mine, :]

    fill_pick(pick, 0, M_DEV)
    own[...] = halves(
        mm(two_terms(by_level(across(64), forth, traces())), pick[...], NT)
    )
    loads[7].wait()
    rows2 = iota((M_DEV, 128), 0)
    for b in range(SLOTS // 128):
        hot = jnp.where(rows2 == slot[b : b + 1, :], 1.0, 0.0).astype(BF16)
        pick2[:, b * 128 : (b + 1) * 128] = hot

    turned_small = small[...].T[0:8]
    for which in range(3):
        wide = widened(turned_small, which)
        ma[24 + 8 * which : 32 + 8 * which, :] = wide[:, 0:192]
        mb[24 + 8 * which : 32 + 8 * which, :] = wide[:, 192:384]
    backward = three_terms(jnp.concatenate([kron(r + 3, s + 3) for r, s in pairs], axis=0))

    slot_row = jnp.concatenate([slot[b : b + 1, :] for b in range(3)], axis=1)
    for b in range(3):
        column = jnp.broadcast_to(slot[b : b + 1, :], (128, 128)).T
        column = jnp.concatenate([column] * 3, axis=1)
        same[128 * b : 128 * b + 128, :] = jnp.where(column == slot_row, 1.0, 0.0).astype(BF16)

    answers[...] = halves(mm(two_terms(own[...]), pick2[...]))
    for copy in group_round:
        copy.wait()
    group_in = recv_g[...]
    coarse_sum = group_in[0:16]
    for i in range(1, GROUP):
        coarse_sum = coarse_sum + group_in[16 * i : 16 * i + 16]
    send_c[0] = coarse_sum
    send_c[1] = coarse_sum
    coarse_round = edge_copies(send_c, recv_c, sc_sem, rc_sem)
    for copy in coarse_round:
        copy.start()
    arrived[:, 256:384] = two_terms(group_in.T[0:64])
    for copy in edge_round:
        copy.wait()
    arrived[:, 0:256] = two_terms(jnp.concatenate([recv_e[0], recv_e[1]], axis=1))
    answer = answers[...] + halves(mm(arrived[...], same[...]))
    send_e2[0] = answer[:, 0:128]
    send_e2[1] = answer[:, 128:256]
    edge_round = edge_copies(send_e2, recv_e2, se2_sem, re2_sem)
    for copy in edge_round:
        copy.start()
    shifted = pltpu.roll(answer[:, 256:384], 120, 1)
    turned = jnp.concatenate([answer[:, 256:384], shifted], axis=0).T
    for i in range(GROUP):
        send_g2[8 * i : 8 * i + 8, :] = turned[16 * i : 16 * i + 8, :]
    group_round = group_copies(send_g2, recv_g2, sg2_sem, rg2_sem, CAP_C // 2)
    for copy in group_round:
        copy.start()
    mine2 = pl.ds(pl.multiple_of(c * 8, 8), 8)
    recv_g2[mine2, :] = send_g2[mine2, :]

    loads[8].wait()
    d_first = first_kron(2)
    d_second = second_kron(2)
    fore12 = three_terms(jnp.concatenate([d_first, d_second], axis=0))
    fore0 = fore12[0:64]
    t_first = three_terms(first_kron(5))
    t_second = three_terms(second_kron(5))
    for j in range(8):
        part = jnp.concatenate(
            [node_rows(u, slice(64 * i + 8 * j, 64 * i + 8 * j + 8)) for i in range(8)], axis=0
        )
        grad = mm(fore0, stacked(part))
        for i in range(8):
            grad0[64 * i + 8 * j : 64 * i + 8 * j + 8, :] = grad[8 * i : 8 * i + 8]
    for i in range(8):
        block = slice(64 * i, 64 * i + 64)
        grad = mm(fore12, stacked(node_rows(u, block)))
        flow1 = met[1, block, :].astype(F32) * grad[0:64]
        flow2 = met[2, block, :].astype(F32) * grad[64:128]
        grad0[block, :] = met[0, block, :].astype(F32) * grad0[block, :]
        back = mm(t_first, stacked(flow1)) + mm(t_second, stacked(flow2))
        acc[0, block, :] = back[:, 0:128]
        acc[1, block, :] = back[:, 128:256]
    for j in range(8):
        part = jnp.concatenate(
            [grad0[64 * i + 8 * j : 64 * i + 8 * j + 8, :] for i in range(8)], axis=0
        )
        back = mm(t_first, stacked(part))
        for i in range(8):
            add_rows(slice(64 * i + 8 * j, 64 * i + 8 * j + 8), back[8 * i : 8 * i + 8])

    mortar = own[...] + halves(mm(arrived[...], pick2[...], NT))
    picked = halves(mm(two_terms(mortar), pick[...]))
    faces[...] = by_level(across(64), backward, picked)

    for copy in coarse_round:
        copy.wait()
    before = recv_c[0]
    after = recv_c[1]

    def widen(mid, left, right):
        near = jnp.where(
            iota((8, 128), 0) < 4, pltpu.roll(left, 4, 0), pltpu.roll(right, 4, 0)
        )
        return jnp.where(iota((8, 128), 1) >= 64, mid + near, 0.0)

    totals = widen(coarse_sum[0:8], before[0:8], after[0:8])
    counts = widen(coarse_sum[8:16], before[8:16], after[8:16])
    coarse = totals / (1.0 + counts)
    coarse_hi = coarse.astype(BF16).astype(F32)
    coarse2 = jnp.concatenate([coarse_hi, coarse - coarse_hi], axis=0).astype(BF16)
    spread = mm(coarse2, corner_hot[...])
    spread = spread[0:8] + spread[8:16]

    for corner in range(8):
        row = 7 * (64 * (corner // 4) + 8 * (corner // 2 % 2) + corner % 2)
        here = eight == high[corner : corner + 1, :]
        fix = jnp.where(here, spread[:, corner * 256 : (corner + 1) * 256], 0.0)
        add_rows(slice(row, row + 1), jnp.sum(fix, axis=0, keepdims=True))
    for copy in group_round:
        copy.wait()
    turned = jnp.concatenate(
        [recv_g2[8 * (i // 2) : 8 * (i // 2) + 8, :] for i in range(2 * GROUP)], axis=0
    ).T
    odd = (iota((64, 128), 1) & 8) != 0
    value = jnp.where(odd, turned[64:128], turned[0:64])
    returned[:, 256:384] = two_terms(by_level(slot_level[:, 256:384], backward, value))

    for copy in edge_round:
        copy.wait()
    value = jnp.concatenate([recv_e2[0], recv_e2[1]], axis=1)
    returned[:, 0:256] = two_terms(by_level(slot_level[:, 0:256], backward, value))


def write(acc, faces, returned, sent, out, buf, sem):
    copies = []
    for side in range(2):
        span = slice(768 * side, 768 * side + 768)
        total = faces[:, span] + halves(mm(returned[...], sent[:, span]))
        for i in range(8):
            rows = slice(64 * i, 64 * i + 64)
            block = acc[side, rows, :]
            if i == 0:
                block = block + total[:, 0:128]
            if i == 7:
                block = block + total[:, 128:256]
            near = block[0:8] + total[8 * i : 8 * i + 8, 256:384]
            away = block[56:64] + total[8 * i : 8 * i + 8, 384:512]
            buf[side, rows, :] = jnp.concatenate([near, block[8:56], away], axis=0)
        for first, part in ((0, total[:, 512:640]), (7, total[:, 640:768])):
            rows = pl.ds(first, 64, stride=8)
            buf[side, rows, :] = buf[side, rows, :] + part
        copy = pltpu.make_async_copy(
            buf.at[side], out.at[:, 128 * side : 128 * side + 128], sem.at[side]
        )
        copy.start()
        copies.append(copy)
    for copy in copies:
        copy.wait()


def on_device(n_elem, nodal, metric, derivative, interp, face_level, face_target, slot_mortar, vertex_ids):
    anywhere = pl.BlockSpec(memory_space=pltpu.HBM)
    dma = pltpu.SemaphoreType.DMA
    parts = pl.pallas_call(
        functools.partial(kernel, n_elem),
        out_shape=[
            jax.ShapeDtypeStruct((2, NODES, 128), F32),
            jax.ShapeDtypeStruct((64, FACES), F32),
            jax.ShapeDtypeStruct((128, SLOTS), BF16),
            jax.ShapeDtypeStruct((SLOTS, FACES), BF16),
        ],
        in_specs=[anywhere] * 8,
        out_specs=[pl.BlockSpec(memory_space=pltpu.VMEM)] * 4,
        scratch_shapes=[
            pltpu.VMEM((2, NODES, 128), F32),
            pltpu.VMEM((3, NODES, E_DEV), BF16),
            pltpu.VMEM((8, 8), F32),
            pltpu.VMEM((2, 8, 8), F32),
            pltpu.VMEM((128, 128), F32),
            pltpu.VMEM((48, 192), F32),
            pltpu.VMEM((48, 192), F32),
            pltpu.VMEM((12, 128), jnp.int32),
            pltpu.VMEM((12, 128), jnp.int32),
            pltpu.VMEM((3, 128), jnp.int32),
            pltpu.VMEM((8, E_DEV), jnp.int32),
            pltpu.VMEM((M_DEV, FACES), BF16),
            pltpu.VMEM((M_DEV, SLOTS), BF16),
            pltpu.VMEM((128, 8 * E_DEV), BF16),
            pltpu.VMEM((144, FACES), BF16),
            pltpu.VMEM((64, SLOTS), F32),
            pltpu.VMEM((64, M_DEV), F32),
            pltpu.VMEM((64, SLOTS), F32),
            pltpu.VMEM((128, SLOTS), BF16),
            pltpu.VMEM((SLOTS, SLOTS), BF16),
            pltpu.VMEM((NODES, E_DEV), F32),
            pltpu.VMEM((2, 64, 128), F32),
            pltpu.VMEM((128, 128), F32),
            pltpu.VMEM((2, 64, 128), F32),
            pltpu.VMEM((128, 128), F32),
            pltpu.VMEM((2, 64, 128), F32),
            pltpu.VMEM((64, 128), F32),
            pltpu.VMEM((2, 64, 128), F32),
            pltpu.VMEM((64, 128), F32),
            pltpu.VMEM((2, 16, 128), F32),
            pltpu.VMEM((2, 16, 128), F32),
            dma((9,)),
            dma((2,)),
            dma((2,)),
            dma((7,)),
            dma((7,)),
            dma((2,)),
            dma((2,)),
            dma((7,)),
            dma((7,)),
            dma((2,)),
            dma((2,)),
        ],
        compiler_params=pltpu.CompilerParams(
            collective_id=0, has_side_effects=True, vmem_limit_bytes=48 * 1024 * 1024
        ),
    )(
        *[
            pltpu.with_memory_space_constraint(x, pltpu.HBM)
            for x in (
                nodal,
                metric,
                derivative,
                interp,
                face_level.reshape(12, 128),
                face_target.reshape(12, 128),
                slot_mortar.reshape(3, 128),
                vertex_ids,
            )
        ]
    )
    return pl.pallas_call(
        write,
        out_shape=jax.ShapeDtypeStruct((NODES, E_DEV), F32),
        in_specs=[pl.BlockSpec(memory_space=pltpu.VMEM)] * 4,
        out_specs=pl.BlockSpec(memory_space=pltpu.HBM),
        scratch_shapes=[pltpu.VMEM((2, NODES, 128), F32), dma((2,))],
    )(*[pltpu.with_memory_space_constraint(part, pltpu.VMEM) for part in parts])


def solution(mesh):
    in_specs = (
        P(None, ("elem", "clus")),
        P(None, None, ("elem", "clus")),
        P(),
        P(),
        P(("elem", "clus")),
        P(("elem", "clus")),
        P(("elem", "clus")),
        P(None, ("elem", "clus")),
    )
    return jax.shard_map(
        functools.partial(on_device, mesh.shape["elem"]),
        mesh=mesh,
        in_specs=in_specs,
        out_specs=P(None, ("elem", "clus")),
        check_vma=False,
    )
```

```python
import functools

import jax
import jax.numpy as jnp
from jax import lax
from jax.experimental import pallas as pl
from jax.experimental.pallas import tpu as pltpu
from jax.sharding import PartitionSpec as P

CAP_E = 128
CAP_C = 16
GROUP = 8
M_DEV = 512
SLOTS = 2 * CAP_E + GROUP * CAP_C
COLS = M_DEV + SLOTS
NV_DEV = 256
E_DEV = 256
FACES = 6 * E_DEV
NODES = 512
MESH = pl.DeviceIdType.MESH
F32 = jnp.float32
BF16 = jnp.bfloat16

NT = (((1,), (1,)), ((), ()))
NN = (((1,), (0,)), ((), ()))


def mm(a, b, dims=NN):
    return lax.dot_general(a, b, dims, preferred_element_type=F32)


def split(x):
    hi = x.astype(BF16)
    return hi, (x - hi.astype(F32)).astype(BF16)


def stacked(x):
    hi, lo = split(x)
    return jnp.concatenate([hi, lo, hi], axis=0)


def halves(x):
    return x[:64] + x[64:]


def two_terms(x):
    hi, lo = split(x)
    return jnp.concatenate([hi, lo], axis=0)


def iota(shape, axis):
    return lax.broadcasted_iota(jnp.int32, shape, axis)


def three_terms(full):
    hi = full.astype(BF16).astype(F32)
    lane = iota(full.shape, 1)
    return jnp.where(lane < 128, hi, full - hi).astype(BF16)


def kernel(
    n_elem,
    u_hbm,
    met_hbm,
    deriv_hbm,
    interp_hbm,
    lvl_hbm,
    tgt_hbm,
    slot_hbm,
    vid_hbm,
    acc,
    faces,
    returned,
    sent,
    u,
    met,
    deriv,
    interp,
    small,
    ma,
    mb,
    lvl,
    tgt,
    slot,
    vid,
    pick,
    pick2,
    corner_hot,
    terms,
    slot_level,
    own,
    answers,
    arrived,
    same,
    grad0,
    send_e,
    send_g,
    recv_e,
    recv_g,
    send_e2,
    send_g2,
    recv_e2,
    recv_g2,
    send_c,
    recv_c,
    in_sem,
    se_sem,
    re_sem,
    sg_sem,
    rg_sem,
    se2_sem,
    re2_sem,
    sg2_sem,
    rg2_sem,
    sc_sem,
    rc_sem,
):
    e = lax.axis_index("elem")
    c = lax.axis_index("clus")
    nxt = lax.rem(e + 1, n_elem)
    prv = lax.rem(e + n_elem - 1, n_elem)

    loads = [
        pltpu.make_async_copy(src, dst, in_sem.at[n])
        for n, (src, dst) in enumerate(
            [
                (tgt_hbm, tgt),
                (u_hbm.at[:, 0:128], u.at[0]),
                (u_hbm.at[:, 128:256], u.at[1]),
                (interp_hbm, interp),
                (deriv_hbm, deriv),
                (lvl_hbm, lvl),
                (vid_hbm, vid),
                (slot_hbm, slot),
                (met_hbm, met),
            ]
        )
    ]
    for load in loads[:8]:
        load.start()

    barrier = pltpu.get_barrier_semaphore()
    for peer in (nxt, prv):
        pl.semaphore_signal(barrier, inc=1, device_id={"elem": peer}, device_id_type=MESH)
    for k in range(1, GROUP):
        peer = lax.rem(c + k, GROUP)
        pl.semaphore_signal(barrier, inc=1, device_id={"clus": peer}, device_id_type=MESH)

    def node_rows(ref, place):
        return jnp.concatenate([ref[0, place, :], ref[1, place, :]], axis=1)

    def add_rows(place, value):
        for side in range(2):
            acc[side, place, :] = acc[side, place, :] + value[:, 128 * side : 128 * side + 128]

    def fill_pick(ref, first, last):
        rows = iota((last - first, 128), 0) + first
        for side in range(2):
            for f in range(6):
                row = 2 * f + side
                place = 128 * (6 * side + f)
                hot = jnp.where(rows == tgt[row : row + 1, :], 1.0, 0.0).astype(BF16)
                ref[:, place : place + 128] = hot

    small[...] = jnp.zeros_like(small)
    for load in loads[:7]:
        load.wait()
    loads[8].start()
    fill_pick(sent, M_DEV, COLS)

    small[0:8, 0:8] = interp[0]
    small[8:16, 0:8] = interp[1]
    small[16:24, 0:8] = deriv[...]
    lane = iota((128, 384), 1)
    inner = jnp.where(lane < 192, (lane & 63) >> 3, lane & 7)

    def widened(x, which):
        spread = jnp.where(iota((128, 384), 0) == inner + 8 * which, 1.0, 0.0)
        return jnp.dot(x, spread, precision=lax.Precision.HIGHEST, preferred_element_type=F32)

    wide = widened(small[0:24, :], 0)
    ma[0:24, :] = wide[:, 0:192]
    mb[0:24, :] = wide[:, 192:384]

    def kron(first, second):
        return jnp.concatenate(
            [
                jnp.broadcast_to(ma[8 * first + x : 8 * first + x + 1, :], (8, 192))
                * mb[8 * second : 8 * second + 8, :]
                for x in range(8)
            ],
            axis=0,
        )

    def first_kron(which):
        full = jnp.concatenate(
            [
                jnp.broadcast_to(ma[8 * which + x : 8 * which + x + 1, :], (8, 192))
                for x in range(8)
            ],
            axis=0,
        )
        keep = (iota((64, 192), 0) & 7) == (iota((64, 192), 1) & 7)
        return jnp.where(keep, full, 0.0)

    def second_kron(which):
        full = jnp.concatenate([mb[8 * which : 8 * which + 8, :]] * 8, axis=0)
        keep = (iota((64, 192), 0) >> 3) == ((iota((64, 192), 1) & 63) >> 3)
        return jnp.where(keep, full, 0.0)

    pairs = [(0, 0), (0, 1), (1, 0), (1, 1)]
    forth = three_terms(jnp.concatenate([kron(r, s) for r, s in pairs], axis=0))

    def across(rows):
        order = [2 * f + side for side in range(2) for f in range(6)]
        row = jnp.concatenate([lvl[n : n + 1, :] for n in order], axis=1)
        return jnp.broadcast_to(row, (rows, FACES))

    def by_level(level, mats, value):
        every = mm(mats, stacked(value))
        chosen = value
        for n in range(4):
            chosen = jnp.where(level == n + 1, every[64 * n : 64 * n + 64], chosen)
        return chosen

    far = [slice(8 * j, 8 * j + 8) for j in range(64)]
    def traces():
        parts = []
        for side in range(2):
            parts += [
                u[side, 0:64, :],
                u[side, 448:512, :],
                jnp.concatenate([u[side, far[8 * i], :] for i in range(8)], axis=0),
                jnp.concatenate([u[side, far[8 * i + 7], :] for i in range(8)], axis=0),
                u[side, pl.ds(0, 64, stride=8), :],
                u[side, pl.ds(7, 64, stride=8), :],
            ]
        return jnp.concatenate(parts, axis=1)

    terms[0:128, :] = two_terms(traces())
    terms[128:144, :] = across(16).astype(F32).astype(BF16)

    away = vid[...] - e * NV_DEV
    total_vertices = n_elem * NV_DEV
    window = jnp.where(away < 0, away + total_vertices, away)
    high = window >> 6
    low = window & 63
    sums = jnp.zeros((32, 128), F32)
    eight = iota((8, E_DEV), 0)
    lanes_rows = iota((128, E_DEV), 0) - 64
    for corner in range(8):
        row = 7 * (64 * (corner // 4) + 8 * (corner // 2 % 2) + corner % 2)
        value = jnp.broadcast_to(node_rows(u, slice(row, row + 1)), (8, E_DEV))
        hi = value.astype(BF16).astype(F32)
        here = eight == high[corner : corner + 1, :]
        parts = [
            jnp.where(here, hi, 0.0),
            jnp.where(here, value - hi, 0.0),
            jnp.where(here, 1.0, 0.0),
            jnp.zeros((8, E_DEV), F32),
        ]
        hot = jnp.where(lanes_rows == low[corner : corner + 1, :], 1.0, 0.0).astype(BF16)
        corner_hot[:, corner * 256 : (corner + 1) * 256] = hot
        sums = sums + mm(jnp.concatenate(parts, axis=0).astype(BF16), hot, NT)
    local = jnp.concatenate([sums[0:8] + sums[8:16], sums[16:24]], axis=0)

    raw = mm(terms[...], sent[...], NT)
    slot_level[...] = jnp.broadcast_to(raw[128:129], (64, SLOTS))
    leaving = by_level(slot_level[...], forth, halves(raw[0:128]))
    send_e[0] = leaving[:, 0:128]
    send_e[1] = leaving[:, 128:256]
    turned = jnp.concatenate([leaving[:, 256:384], jnp.zeros((64, 128), F32)], axis=0).T
    send_g[...] = turned + jnp.concatenate([local] * GROUP, axis=0)

    def edge_copies(src, dst, ssem, rsem):
        return [
            pltpu.make_async_remote_copy(
                src.at[way],
                dst.at[1 - way],
                ssem.at[way],
                rsem.at[1 - way],
                device_id={"elem": peer},
                device_id_type=MESH,
            )
            for way, peer in ((0, prv), (1, nxt))
        ]

    def group_copies(src, dst, ssem, rsem, rows):
        copies = []
        for k in (4, 5, 3, 2, 6, 7, 1):
            peer = lax.rem(c + k, GROUP)
            copies.append(
                pltpu.make_async_remote_copy(
                    src.at[pl.ds(pl.multiple_of(peer * rows, rows), rows), :],
                    dst.at[pl.ds(pl.multiple_of(c * rows, rows), rows), :],
                    ssem.at[k - 1],
                    rsem.at[k - 1],
                    device_id={"clus": peer},
                    device_id_type=MESH,
                )
            )
        return copies

    pl.semaphore_wait(barrier, GROUP + 1)
    edge_round = edge_copies(send_e, recv_e, se_sem, re_sem)
    group_round = group_copies(send_g, recv_g, sg_sem, rg_sem, CAP_C)
    for copy in edge_round + group_round:
        copy.start()
    mine = pl.ds(pl.multiple_of(c * CAP_C, CAP_C), CAP_C)
    recv_g[mine, :] = send_g[mine, :]

    fill_pick(pick, 0, M_DEV)
    own[...] = halves(
        mm(two_terms(by_level(across(64), forth, traces())), pick[...], NT)
    )
    loads[7].wait()
    rows2 = iota((M_DEV, 128), 0)
    for b in range(SLOTS // 128):
        hot = jnp.where(rows2 == slot[b : b + 1, :], 1.0, 0.0).astype(BF16)
        pick2[:, b * 128 : (b + 1) * 128] = hot

    turned_small = small[...].T[0:8]
    for which in range(3):
        wide = widened(turned_small, which)
        ma[24 + 8 * which : 32 + 8 * which, :] = wide[:, 0:192]
        mb[24 + 8 * which : 32 + 8 * which, :] = wide[:, 192:384]
    backward = three_terms(jnp.concatenate([kron(r + 3, s + 3) for r, s in pairs], axis=0))

    slot_row = jnp.concatenate([slot[b : b + 1, :] for b in range(3)], axis=1)
    for b in range(3):
        column = jnp.broadcast_to(slot[b : b + 1, :], (128, 128)).T
        column = jnp.concatenate([column] * 3, axis=1)
        same[128 * b : 128 * b + 128, :] = jnp.where(column == slot_row, 1.0, 0.0).astype(BF16)

    answers[...] = halves(mm(two_terms(own[...]), pick2[...]))
    for copy in group_round:
        copy.wait()
    group_in = recv_g[...]
    coarse_sum = group_in[0:16]
    for i in range(1, GROUP):
        coarse_sum = coarse_sum + group_in[16 * i : 16 * i + 16]
    send_c[0] = coarse_sum
    send_c[1] = coarse_sum
    coarse_round = edge_copies(send_c, recv_c, sc_sem, rc_sem)
    for copy in coarse_round:
        copy.start()
    arrived[:, 256:384] = two_terms(group_in.T[0:64])
    for copy in edge_round:
        copy.wait()
    arrived[:, 0:256] = two_terms(jnp.concatenate([recv_e[0], recv_e[1]], axis=1))
    answer = answers[...] + halves(mm(arrived[...], same[...]))
    send_e2[0] = answer[:, 0:128]
    send_e2[1] = answer[:, 128:256]
    edge_round = edge_copies(send_e2, recv_e2, se2_sem, re2_sem)
    for copy in edge_round:
        copy.start()
    shifted = pltpu.roll(answer[:, 256:384], 120, 1)
    turned = jnp.concatenate([answer[:, 256:384], shifted], axis=0).T
    for i in range(GROUP):
        send_g2[8 * i : 8 * i + 8, :] = turned[16 * i : 16 * i + 8, :]
    group_round = group_copies(send_g2, recv_g2, sg2_sem, rg2_sem, CAP_C // 2)
    for copy in group_round:
        copy.start()
    mine2 = pl.ds(pl.multiple_of(c * 8, 8), 8)
    recv_g2[mine2, :] = send_g2[mine2, :]

    loads[8].wait()
    d_first = first_kron(2)
    d_second = second_kron(2)
    fore12 = three_terms(jnp.concatenate([d_first, d_second], axis=0))
    fore0 = fore12[0:64]
    t_first = three_terms(first_kron(5))
    t_second = three_terms(second_kron(5))
    for j in range(8):
        part = jnp.concatenate(
            [node_rows(u, slice(64 * i + 8 * j, 64 * i + 8 * j + 8)) for i in range(8)], axis=0
        )
        grad = mm(fore0, stacked(part))
        for i in range(8):
            grad0[64 * i + 8 * j : 64 * i + 8 * j + 8, :] = grad[8 * i : 8 * i + 8]
    for i in range(8):
        block = slice(64 * i, 64 * i + 64)
        grad = mm(fore12, stacked(node_rows(u, block)))
        flow1 = met[1, block, :].astype(F32) * grad[0:64]
        flow2 = met[2, block, :].astype(F32) * grad[64:128]
        grad0[block, :] = met[0, block, :].astype(F32) * grad0[block, :]
        back = mm(t_first, stacked(flow1)) + mm(t_second, stacked(flow2))
        acc[0, block, :] = back[:, 0:128]
        acc[1, block, :] = back[:, 128:256]
    for j in range(8):
        part = jnp.concatenate(
            [grad0[64 * i + 8 * j : 64 * i + 8 * j + 8, :] for i in range(8)], axis=0
        )
        back = mm(t_first, stacked(part))
        for i in range(8):
            add_rows(slice(64 * i + 8 * j, 64 * i + 8 * j + 8), back[8 * i : 8 * i + 8])

    mortar = own[...] + halves(mm(arrived[...], pick2[...], NT))
    picked = halves(mm(two_terms(mortar), pick[...]))
    faces[...] = by_level(across(64), backward, picked)

    for copy in coarse_round:
        copy.wait()
    before = recv_c[0]
    after = recv_c[1]

    def widen(mid, left, right):
        near = jnp.where(
            iota((8, 128), 0) < 4, pltpu.roll(left, 4, 0), pltpu.roll(right, 4, 0)
        )
        return jnp.where(iota((8, 128), 1) >= 64, mid + near, 0.0)

    totals = widen(coarse_sum[0:8], before[0:8], after[0:8])
    counts = widen(coarse_sum[8:16], before[8:16], after[8:16])
    coarse = totals / (1.0 + counts)
    coarse_hi = coarse.astype(BF16).astype(F32)
    coarse2 = jnp.concatenate([coarse_hi, coarse - coarse_hi], axis=0).astype(BF16)
    spread = mm(coarse2, corner_hot[...])
    spread = spread[0:8] + spread[8:16]

    for corner in range(8):
        row = 7 * (64 * (corner // 4) + 8 * (corner // 2 % 2) + corner % 2)
        here = eight == high[corner : corner + 1, :]
        fix = jnp.where(here, spread[:, corner * 256 : (corner + 1) * 256], 0.0)
        add_rows(slice(row, row + 1), jnp.sum(fix, axis=0, keepdims=True))
    for copy in group_round:
        copy.wait()
    turned = jnp.concatenate(
        [recv_g2[8 * (i // 2) : 8 * (i // 2) + 8, :] for i in range(2 * GROUP)], axis=0
    ).T
    odd = (iota((64, 128), 1) & 8) != 0
    value = jnp.where(odd, turned[64:128], turned[0:64])
    returned[:, 256:384] = two_terms(by_level(slot_level[:, 256:384], backward, value))

    for copy in edge_round:
        copy.wait()
    value = jnp.concatenate([recv_e2[0], recv_e2[1]], axis=1)
    returned[:, 0:256] = two_terms(by_level(slot_level[:, 0:256], backward, value))


def write(acc, faces, returned, sent, out, buf, sem):
    copies = []
    for side in range(2):
        span = slice(768 * side, 768 * side + 768)
        total = faces[:, span] + halves(mm(returned[...], sent[:, span]))
        for quarter in range(2):
            for i in range(4 * quarter, 4 * quarter + 4):
                rows = slice(64 * i, 64 * i + 64)
                block = acc[side, rows, :]
                if i == 0:
                    block = block + total[:, 0:128]
                if i == 7:
                    block = block + total[:, 128:256]
                near = block[0:8] + total[8 * i : 8 * i + 8, 256:384]
                away = block[56:64] + total[8 * i : 8 * i + 8, 384:512]
                buf[side, rows, :] = jnp.concatenate([near, block[8:56], away], axis=0)
            half = slice(32 * quarter, 32 * quarter + 32)
            for first, part in ((0, total[half, 512:640]), (7, total[half, 640:768])):
                rows = pl.ds(256 * quarter + first, 32, stride=8)
                buf[side, rows, :] = buf[side, rows, :] + part
            rows = slice(256 * quarter, 256 * quarter + 256)
            copy = pltpu.make_async_copy(
                buf.at[side, rows],
                out.at[rows, 128 * side : 128 * side + 128],
                sem.at[2 * side + quarter],
            )
            copy.start()
            copies.append(copy)
    for copy in copies:
        copy.wait()


def on_device(n_elem, nodal, metric, derivative, interp, face_level, face_target, slot_mortar, vertex_ids):
    anywhere = pl.BlockSpec(memory_space=pltpu.HBM)
    dma = pltpu.SemaphoreType.DMA
    parts = pl.pallas_call(
        functools.partial(kernel, n_elem),
        out_shape=[
            jax.ShapeDtypeStruct((2, NODES, 128), F32),
            jax.ShapeDtypeStruct((64, FACES), F32),
            jax.ShapeDtypeStruct((128, SLOTS), BF16),
            jax.ShapeDtypeStruct((SLOTS, FACES), BF16),
        ],
        in_specs=[anywhere] * 8,
        out_specs=[pl.BlockSpec(memory_space=pltpu.VMEM)] * 4,
        scratch_shapes=[
            pltpu.VMEM((2, NODES, 128), F32),
            pltpu.VMEM((3, NODES, E_DEV), BF16),
            pltpu.VMEM((8, 8), F32),
            pltpu.VMEM((2, 8, 8), F32),
            pltpu.VMEM((128, 128), F32),
            pltpu.VMEM((48, 192), F32),
            pltpu.VMEM((48, 192), F32),
            pltpu.VMEM((12, 128), jnp.int32),
            pltpu.VMEM((12, 128), jnp.int32),
            pltpu.VMEM((3, 128), jnp.int32),
            pltpu.VMEM((8, E_DEV), jnp.int32),
            pltpu.VMEM((M_DEV, FACES), BF16),
            pltpu.VMEM((M_DEV, SLOTS), BF16),
            pltpu.VMEM((128, 8 * E_DEV), BF16),
            pltpu.VMEM((144, FACES), BF16),
            pltpu.VMEM((64, SLOTS), F32),
            pltpu.VMEM((64, M_DEV), F32),
            pltpu.VMEM((64, SLOTS), F32),
            pltpu.VMEM((128, SLOTS), BF16),
            pltpu.VMEM((SLOTS, SLOTS), BF16),
            pltpu.VMEM((NODES, E_DEV), F32),
            pltpu.VMEM((2, 64, 128), F32),
            pltpu.VMEM((128, 128), F32),
            pltpu.VMEM((2, 64, 128), F32),
            pltpu.VMEM((128, 128), F32),
            pltpu.VMEM((2, 64, 128), F32),
            pltpu.VMEM((64, 128), F32),
            pltpu.VMEM((2, 64, 128), F32),
            pltpu.VMEM((64, 128), F32),
            pltpu.VMEM((2, 16, 128), F32),
            pltpu.VMEM((2, 16, 128), F32),
            dma((9,)),
            dma((2,)),
            dma((2,)),
            dma((7,)),
            dma((7,)),
            dma((2,)),
            dma((2,)),
            dma((7,)),
            dma((7,)),
            dma((2,)),
            dma((2,)),
        ],
        compiler_params=pltpu.CompilerParams(
            collective_id=0, has_side_effects=True, vmem_limit_bytes=48 * 1024 * 1024
        ),
    )(
        *[
            pltpu.with_memory_space_constraint(x, pltpu.HBM)
            for x in (
                nodal,
                metric,
                derivative,
                interp,
                face_level.reshape(12, 128),
                face_target.reshape(12, 128),
                slot_mortar.reshape(3, 128),
                vertex_ids,
            )
        ]
    )
    return pl.pallas_call(
        write,
        out_shape=jax.ShapeDtypeStruct((NODES, E_DEV), F32),
        in_specs=[pl.BlockSpec(memory_space=pltpu.VMEM)] * 4,
        out_specs=pl.BlockSpec(memory_space=pltpu.HBM),
        scratch_shapes=[pltpu.VMEM((2, NODES, 128), F32), dma((4,))],
    )(*[pltpu.with_memory_space_constraint(part, pltpu.VMEM) for part in parts])


def solution(mesh):
    in_specs = (
        P(None, ("elem", "clus")),
        P(None, None, ("elem", "clus")),
        P(),
        P(),
        P(("elem", "clus")),
        P(("elem", "clus")),
        P(("elem", "clus")),
        P(None, ("elem", "clus")),
    )
    return jax.shard_map(
        functools.partial(on_device, mesh.shape["elem"]),
        mesh=mesh,
        in_specs=in_specs,
        out_specs=P(None, ("elem", "clus")),
        check_vma=False,
    )
```
